256 devices in a mesh: tile: 16 (over z_lo, y, core), quad: 16 (over z_hi, x).
Axes of the slice: x: 4, y: 4, z: 8 (z_hi: 4, z_lo: 2; z = z_hi * 2 + z_lo), core: 2. Of those that a mesh axis runs over, the one named last changes fastest.
Arguments:
- adjoint_next: float32 [32, 32, 2048], P('quad', None, 'tile'), may hold values from -6 to 6
- saved_state: float32 [32, 32, 2048], P('quad', None, 'tile'), may hold values from 0.2 to 2
- gain_left: float32 [16, 32, 1024], P('quad'), may hold values from 0.1 to 2
- gain_right: float32 [16, 32, 1024], P('quad'), may hold values from 0.1 to 2
Outputs:
- adjoint_prev: float32 [32, 32, 2048], P('quad', None, 'tile')
The draws below stay inside these ranges and needn't reach their ends.
All inputs are finite; a program needn't handle non-finite values.
Results may differ from the reference program's by a relative error of at most 0.0001.
Values sent between devices are 32-bit elements; how exact they have to be, the bound alone decides.
A program may use at most 64 MiB of HBM per device.

```python
import math
import jax
import jax.numpy as jnp
from jax import lax

NV = 32
CY = 2
PAIRS = 16
NXC = 32


def shard_levels(own_key, shape, split, least, high):
    factor_of, own = 1.0, jax.random.fold_in(own_key, 6)
    for position, parts in split:
        steps = jnp.exp(jax.random.uniform(jax.random.fold_in(own, position), (parts,), jnp.float32, least / len(split), high / len(split)))
        factor_of = factor_of * jnp.repeat(steps, shape[position] // parts).reshape([-1 if axis == position else 1 for axis in range(len(shape))])
    return factor_of


def centred(stream_key, extent, deviation, most, cuts=(), kind=jnp.bfloat16):
    entries = jax.random.normal(stream_key, extent, jnp.float32) * deviation
    if len(cuts) > 0:
        entries = shard_levels(stream_key, extent, cuts, -0.22, 0.18) * entries
    return jnp.clip(entries, min=-most, max=most).astype(kind)


def setup_inputs(seed: int = 0) -> dict:
    key_list = jax.random.split(jax.random.key(seed), 5)
    adjoint_next = centred(key_list[0], (NV, NV, NXC * CY * NV), 1.0, 6.0, ((0, 16), (2, 16)), jnp.float32)
    saved_state = jnp.clip(0.2 + 1.8 * jax.random.uniform(key_list[1], (NV, NV, NXC * CY * NV), jnp.float32) ** shard_levels(key_list[1], (NV, NV, NXC * CY * NV), ((0, 16), (2, 16)), -0.2, 0.2), 0.2, 2.0)
    gain_left = jnp.clip(jnp.exp(math.log(2.0) - 2.9957323 * jax.random.uniform(key_list[2], (PAIRS, NV, NV * NV), jnp.float32) ** shard_levels(key_list[2], (PAIRS, NV, NV * NV), ((0, 16),), -0.2, 0.2)), 0.1, 2.0)
    gain_right = jnp.clip(jnp.exp(math.log(2.0) - 2.9957323 * jax.random.uniform(key_list[3], (PAIRS, NV, NV * NV), jnp.float32) ** shard_levels(key_list[3], (PAIRS, NV, NV * NV), ((0, 16),), -0.2, 0.2)), 0.1, 2.0)
    return dict(adjoint_next=adjoint_next, saved_state=saved_state, gain_left=gain_left, gain_right=gain_right)


def stream_axis(values, along, courant):
    ahead_one = jnp.roll(values, -1, along)
    ahead_two = jnp.roll(values, -2, along)
    behind_one = jnp.roll(values, 1, along)
    behind_two = jnp.roll(values, 2, along)
    upwind = jnp.maximum(courant, 0.0) * (3.0 * values - 4.0 * ahead_one + ahead_two) / 2.0
    downwind = jnp.minimum(courant, 0.0) * (3.0 * values - 4.0 * behind_one + behind_two) / 2.0
    return downwind - upwind


def even_half(multiplier):
    flip_axes = (0, 1, 2)
    mirrored = jnp.roll(jnp.flip(multiplier, flip_axes), 1, flip_axes)
    return ((multiplier + mirrored) * 0.5)[:, :, : NV // 2 + 1]


def reference(adjoint_next, saved_state, gain_left, gain_right):
    adjoint_grid = adjoint_next.reshape(NV, NV, NXC, CY, NV)
    state_grid = saved_state.reshape(NV, NV, NXC, CY, NV)
    speeds = (jnp.arange(NV, dtype=jnp.float32) - (NV - 1) / 2.0) / NV
    courant_x = speeds.reshape(NV, 1, 1, 1, 1)
    courant_y = speeds.reshape(1, NV, 1, 1, 1)
    passed = adjoint_grid + stream_axis(adjoint_grid, 2, courant_x) + stream_axis(adjoint_grid, 3, courant_y)
    cell_count = NXC * CY
    adjoint_cells = jnp.transpose(passed, (2, 3, 0, 1, 4)).reshape(cell_count, NV, NV, NV)
    state_cells = jnp.transpose(state_grid, (2, 3, 0, 1, 4)).reshape(cell_count, NV, NV, NV)
    left_tables = gain_left.reshape(PAIRS, NV, NV, NV)
    right_tables = gain_right.reshape(PAIRS, NV, NV, NV)
    spectral_axes = (1, 2, 3)
    velocity_shape = (NV, NV, NV)
    spectrum = jnp.fft.rfftn(state_cells, axes=spectral_axes)
    product = jnp.fft.rfftn(state_cells * adjoint_cells, axes=spectral_axes)

    def per_pair(totals, pair_items):
        left_full, right_full = pair_items
        left_one = even_half(left_full)
        right_one = even_half(right_full)
        loss_one = even_half(left_full * right_full)
        filtered_left = jnp.fft.irfftn(spectrum * left_one, s=velocity_shape, axes=spectral_axes)
        filtered_right = jnp.fft.irfftn(spectrum * right_one, s=velocity_shape, axes=spectral_axes)
        pair_term = (left_one * jnp.fft.rfftn(adjoint_cells * filtered_right, axes=spectral_axes)
                     + right_one * jnp.fft.rfftn(adjoint_cells * filtered_left, axes=spectral_axes)
                     - loss_one * product)
        return (totals[0] + jnp.real(pair_term), totals[1] + jnp.imag(pair_term)), None

    empty_sum = jnp.zeros(spectrum.shape, jnp.float32)
    (total_real, total_imag), _ = lax.scan(per_pair, (empty_sum, empty_sum), (left_tables, right_tables))
    loss_table = even_half(jnp.sum(left_tables * right_tables, axis=0))
    loss_field = jnp.fft.irfftn(spectrum * loss_table, s=velocity_shape, axes=spectral_axes)
    collision = jnp.fft.irfftn(lax.complex(total_real, total_imag), s=velocity_shape, axes=spectral_axes) - adjoint_cells * loss_field
    result_cells = adjoint_cells + collision / PAIRS
    result_grid = jnp.transpose(result_cells.reshape(NXC, CY, NV, NV, NV), (2, 3, 0, 1, 4))
    return result_grid.reshape(NV, NV, NXC * CY * NV)
```

```python
import functools
import ml_dtypes
import numpy as np
import jax
import jax.numpy as jnp
from jax import lax
from jax.experimental import pallas as pl
from jax.experimental.pallas import tpu as pltpu
from jax.sharding import PartitionSpec as P

MESH = pl.DeviceIdType.MESH
NV = 32
ROOT_HALF = float(np.sqrt(0.5))


def in_real_form(matrix):
    return np.block([[matrix.real, matrix.imag], [-matrix.imag, matrix.real]])


def two_halves(matrix):
    high = matrix.astype(ml_dtypes.bfloat16)
    low = (matrix - high.astype(np.float64)).astype(ml_dtypes.bfloat16)
    return high, low


def make_tables():
    steps = np.arange(NV)
    whole = np.exp(-2j * np.pi * (steps[:, None] * steps[None, :] % NV) / NV)
    four = np.arange(4)
    quarter = np.exp(-2j * np.pi * (four[:, None] * four[None, :] % 4) / 4)
    lanes = np.kron(quarter, whole)
    slots = np.kron(np.eye(4), whole)
    blocks = [
        in_real_form(lanes),
        in_real_form(slots),
        in_real_form(np.tile(whole, (1, 4))),
        in_real_form(slots.conj() / NV),
        in_real_form(lanes.conj() / NV**2),
    ]
    rows = []
    for block in blocks:
        rows.extend(two_halves(block))
    total = in_real_form(np.tile(whole.conj() / NV, (4, 1)))
    total = np.concatenate([total, np.zeros((256, 64))], axis=1)
    rows.append(np.concatenate(two_halves(total), axis=1))
    return np.concatenate(rows, axis=0)


ROWS_OF = {
    "lanes": (0, 256, 256),
    "slots": (512, 768, 256),
    "spread": (1024, 1088, 64),
    "slots_back": (1152, 1408, 256),
    "lanes_back": (1664, 1920, 256),
}
TOTAL_ROW = 2176
TABLE_ROWS = 2432


def split(x):
    high = x.astype(jnp.bfloat16)
    low = (x - high.astype(jnp.float32)).astype(jnp.bfloat16)
    return high, low


def product(x, high, low):
    xh, xl = split(x)
    dot = functools.partial(jnp.dot, preferred_element_type=jnp.float32)
    return dot(xh, high) + dot(xl, high) + dot(xh, low)


def turned(x):
    return jnp.concatenate([x[:, :128].T, x[:, 128:].T], axis=1)


def turn_by(value, factor):
    re, im = value
    fr, fi = factor
    if abs(fi) < 1e-12 and abs(fr - 1.0) < 1e-12:
        return value
    return (re * fr - im * fi, re * fi + im * fr)


def plus(a, b):
    return (a[0] + b[0], a[1] + b[1])


def minus(a, b):
    return (a[0] - b[0], a[1] - b[1])


def four_points(x, sign):
    s0, d0 = plus(x[0], x[2]), minus(x[0], x[2])
    s1, d1 = plus(x[1], x[3]), minus(x[1], x[3])
    side = (-sign * d1[1], sign * d1[0]) if sign > 0 else (d1[1], -d1[0])
    return [plus(s0, s1), plus(d0, side), minus(s0, s1), minus(d0, side)]


def eight_points(x, sign):
    even = four_points(x[0::2], sign)
    odd = four_points(x[1::2], sign)
    o1, o2, o3 = odd[1], odd[2], odd[3]
    if sign < 0:
        o1 = ((o1[0] + o1[1]) * ROOT_HALF, (o1[1] - o1[0]) * ROOT_HALF)
        o2 = (o2[1], -o2[0])
        o3 = ((o3[1] - o3[0]) * ROOT_HALF, (o3[0] + o3[1]) * -ROOT_HALF)
    else:
        o1 = ((o1[0] - o1[1]) * ROOT_HALF, (o1[1] + o1[0]) * ROOT_HALF)
        o2 = (-o2[1], o2[0])
        o3 = ((o3[0] + o3[1]) * -ROOT_HALF, (o3[0] - o3[1]) * ROOT_HALF)
    odd = [odd[0], o1, o2, o3]
    return [plus(e, o) for e, o in zip(even, odd)] + [minus(e, o) for e, o in zip(even, odd)]


def twiddle(index, residue, sign):
    angle = sign * 2.0 * np.pi * (index * residue % NV) / NV
    return float(np.cos(angle)), float(np.sin(angle))


def forward_eight(x, residue):
    return eight_points([turn_by(v, twiddle(n, residue, -1)) for n, v in enumerate(x)], -1)


def backward_eight(x, residue):
    return [turn_by(v, twiddle(n, residue, 1)) for n, v in enumerate(eight_points(x, 1))]


def exchange_lanes(tiles):
    group = lax.broadcasted_iota(jnp.int32, (8, 128), 1) // 32
    upper = group >= 2
    odd = group % 2 == 1
    y = [None] * 4
    for h in range(2):
        y[h] = jnp.where(upper, pltpu.roll(tiles[h + 2], 64, 1), tiles[h])
        y[h + 2] = jnp.where(upper, tiles[h + 2], pltpu.roll(tiles[h], 64, 1))
    z = [None] * 4
    for h in (0, 2):
        z[h] = jnp.where(odd, pltpu.roll(y[h + 1], 32, 1), y[h])
        z[h + 1] = jnp.where(odd, y[h + 1], pltpu.roll(y[h], 96, 1))
    return z


def kernel(
    adjoint,
    state,
    gain_left,
    gain_right,
    table_hbm,
    out,
    table,
    beside,
    passed_own,
    state_sent,
    passed_sent,
    state_all,
    passed_all,
    result,
    arrived,
    gains,
    turned_gains,
    even_left,
    even_right,
    even_loss,
    spectrum,
    product_spectrum,
    work,
    loss_work,
    loss_field,
    local_sem,
    halo_sem,
    state_send,
    state_recv,
    passed_send,
    passed_recv,
    result_send,
    result_recv,
    gain_send,
    gain_recv,
    share_send,
    share_recv,
):
    tile = lax.axis_index("tile")
    quad = lax.axis_index("quad")
    tiles = lax.axis_size("tile")
    column = lax.rem(quad, 4)
    row = quad // 4
    core = lax.rem(tile, 2)
    sibling = tile + 1 - 2 * core
    ahead = quad >= 8
    up, down = lax.rem(tile + 1, tiles), lax.rem(tile + tiles - 1, tiles)
    source_tile = jnp.where(ahead, up, down)
    target_tile = jnp.where(ahead, down, up)

    fetch_table = pltpu.make_async_copy(table_hbm, table, local_sem.at[0])
    fetch_left = pltpu.make_async_copy(
        gain_left.at[0], gains.at[0, pl.ds(column * 32, 32), :], local_sem.at[1]
    )
    fetch_right = pltpu.make_async_copy(
        gain_right.at[0], gains.at[1, pl.ds(column * 32, 32), :], local_sem.at[2]
    )
    fetch_left.start()
    fetch_right.start()
    fetch_table.start()

    barrier = pltpu.get_barrier_semaphore()

    def greet(step, carry):
        peer = lax.rem(quad + step, 16)
        pl.semaphore_signal(barrier, inc=1, device_id={"quad": peer}, device_id_type=MESH)
        return carry

    lax.fori_loop(1, 16, greet, 0)
    pl.semaphore_signal(barrier, inc=1, device_id={"tile": source_tile}, device_id_type=MESH)
    pl.semaphore_signal(barrier, inc=1, device_id={"tile": sibling}, device_id_type=MESH)

    for j in range(2):
        cells = exchange_lanes([state[j, 8 * h : 8 * h + 8, :] for h in range(4)])
        for cell in range(4):
            state_sent[cell, 8 * j : 8 * j + 8, :] = cells[cell]
    state_all[pl.ds(quad * 16, 16), :] = state_sent[column]

    pl.semaphore_wait(barrier, 17)

    halo = pltpu.make_async_remote_copy(
        src_ref=adjoint,
        dst_ref=beside,
        send_sem=halo_sem.at[0],
        recv_sem=halo_sem.at[1],
        device_id={"tile": target_tile},
        device_id_type=MESH,
    )
    halo.start()

    def to_peer(sent, whole, send, recv, peer):
        return pltpu.make_async_remote_copy(
            src_ref=sent.at[lax.rem(peer, 4)],
            dst_ref=whole.at[pl.ds(quad * 16, 16), :],
            send_sem=send.at[peer],
            recv_sem=recv.at[quad],
            device_id={"quad": peer},
            device_id_type=MESH,
        )

    def from_peer(sent, whole, send, recv, peer):
        return pltpu.make_async_remote_copy(
            src_ref=sent.at[0],
            dst_ref=whole.at[pl.ds(peer * 16, 16), :],
            send_sem=send.at[peer],
            recv_sem=recv.at[peer],
            device_id={"quad": peer},
            device_id_type=MESH,
        )

    def for_peers(action):
        def body(step, carry):
            action(lax.rem(quad + step, 16))
            return carry

        lax.fori_loop(1, 16, body, 0)

    state_refs = (state_sent, state_all, state_send, state_recv)
    passed_refs = (passed_sent, passed_all, passed_send, passed_recv)
    for_peers(lambda peer: to_peer(*state_refs, peer).start())

    fetch_left.wait()
    fetch_right.wait()

    def gain_copy(position):
        return pltpu.make_async_remote_copy(
            src_ref=gains.at[core, pl.ds(column * 32, 32), :],
            dst_ref=gains.at[core, pl.ds(column * 32, 32), :],
            send_sem=gain_send.at[position],
            recv_sem=gain_recv.at[column],
            device_id={"quad": row * 4 + position},
            device_id_type=MESH,
        )

    def gain_arrival(position, kind, send, recv):
        return pltpu.make_async_remote_copy(
            src_ref=gains.at[kind, pl.ds(position * 32, 32), :],
            dst_ref=gains.at[kind, pl.ds(position * 32, 32), :],
            send_sem=send.at[position],
            recv_sem=recv.at[position],
            device_id={"tile": sibling},
            device_id_type=MESH,
        )

    for step in (1, 3, 2):
        gain_copy(lax.rem(column + step, 4)).start()

    halo.wait_recv()
    lane = lax.broadcasted_iota(jnp.int32, (8, 128), 1)
    lower = lane < 64
    odd_cell = lane // 32 % 2 == 1
    from_own = jnp.logical_xor(lower, jnp.logical_not(ahead))
    for j in range(2):
        plane = (quad * 2 + j).astype(jnp.float32)
        speed_x = jnp.abs((plane - (NV - 1) / 2.0) / NV)
        for h in range(4):
            rows = slice(8 * h, 8 * h + 8)
            own = adjoint[j, rows, :]
            second = beside[j, rows, :]
            first = jnp.where(from_own, pltpu.roll(own, 64, 1), pltpu.roll(second, 64, 1))
            partner = jnp.where(odd_cell, pltpu.roll(own, 32, 1), pltpu.roll(own, 96, 1))
            b = (lax.broadcasted_iota(jnp.int32, (8, 128), 0) + 8 * h).astype(jnp.float32)
            speed_y = jnp.abs((b - (NV - 1) / 2.0) / NV)
            passed_own[j, rows, :] = (
                own
                - speed_x * (3.0 * own - 4.0 * first + second) * 0.5
                - 2.0 * speed_y * (own - partner)
            )
        cells = exchange_lanes([passed_own[j, 8 * h : 8 * h + 8, :] for h in range(4)])
        for cell in range(4):
            passed_sent[cell, 8 * j : 8 * j + 8, :] = cells[cell]
    passed_all[pl.ds(quad * 16, 16), :] = passed_sent[column]
    for_peers(lambda peer: to_peer(*passed_refs, peer).start())

    def tables(name):
        high, low, count = ROWS_OF[name]
        return table[high : high + count, :], table[low : low + count, :]

    def one_spread(values, store, low_index):
        high, low = tables("lanes")
        mid = product(values, high[:128], low[:128])
        mid = jnp.concatenate([mid[:, :128], mid[:, 128:]], axis=0).T
        store[low_index] = product(mid, *tables("spread"))

    def plane_of(ref, low_index):
        return ref[pl.ds(low_index, 32, stride=8), :]

    fetch_table.wait()
    for_peers(lambda peer: from_peer(*state_refs, peer).wait_recv())

    def state_step(i, carry):
        one_spread(plane_of(state_all, i), spectrum, i)
        return carry

    lax.fori_loop(0, 8, state_step, 0)

    for step in (1, 3, 2):
        position = lax.rem(column + step, 4)
        gain_arrival(position, core, gain_send, gain_recv).wait_recv()
        gain_arrival(position, core, share_send, share_recv).start()
    for step in (1, 3, 2):
        position = lax.rem(column + step, 4)
        gain_arrival(position, 1 - core, share_send, share_recv).wait_recv()

    lanes = lax.broadcasted_iota(jnp.int32, (128, 128), 1)
    mirror_low = lax.rem(4 - lanes // 32, 4) * 32 + lax.rem(32 - lax.rem(lanes, 32), 32)
    mirror_one = lanes // 32 * 32 + lax.rem(32 - lax.rem(lanes, 32), 32)

    def gain_step(h, carry):
        columns = pl.ds(pl.multiple_of(h * 128, 128), 128)
        for kind in range(2):
            block = gains[kind, :, columns]
            turned_gains[kind, h] = block.T
            flipped = jnp.take_along_axis(block, mirror_low, axis=1).T
            turned_gains[2 + kind, h] = jnp.take_along_axis(flipped, mirror_one, axis=1)
        return carry

    lax.fori_loop(0, 8, gain_step, 0)

    def load_eight(ref, rows):
        return [(ref[n, rows, :128], ref[n, rows, 128:]) for n in range(8)]

    def store_eight(ref, rows, values):
        for n, (re, im) in enumerate(values):
            ref[n, rows, :128] = re
            ref[n, rows, 128:] = im

    for residue in range(4):

        def filter_step(r, carry, residue=residue):
            rows = pl.ds(pl.multiple_of(residue * 32 + r * 8, 8), 8)
            whole = forward_eight(load_eight(spectrum, rows), residue)
            both, loss = [], []
            for n, (re, im) in enumerate(whole):
                other = (-n - (1 if residue else 0)) % 8
                left, right = turned_gains[0, n, rows, :], turned_gains[1, n, rows, :]
                left_m, right_m = turned_gains[2, other, rows, :], turned_gains[3, other, rows, :]
                even_l = (left + left_m) * 0.5
                even_r = (right + right_m) * 0.5
                even_c = (left * right + left_m * right_m) * 0.5
                even_left[n, rows, :] = even_l
                even_right[n, rows, :] = even_r
                even_loss[n, rows, :] = even_c
                both.append((even_l * re - even_r * im, even_l * im + even_r * re))
                loss.append((even_c * re, even_c * im))
            store_eight(work, rows, backward_eight(both, residue))
            store_eight(loss_work, rows, backward_eight(loss, residue))
            return carry

        lax.fori_loop(0, 4, filter_step, 0)

    def one_field(low_values):
        half = product(
            low_values,
            table[TOTAL_ROW : TOTAL_ROW + 256, :128],
            table[TOTAL_ROW : TOTAL_ROW + 256, 128:],
        ).T
        half = jnp.concatenate([half[:32], half[32:64]], axis=1)
        high, low = tables("lanes_back")
        return product(half, high[:, :128], low[:, :128])

    def back_step(i, carry):
        half = product(work[i], *tables("slots_back"))
        work[i] = product(turned(half), *tables("lanes_back"))
        loss_field[i] = one_field(loss_work[i])
        return carry

    lax.fori_loop(0, 8, back_step, 0)

    for_peers(lambda peer: from_peer(*passed_refs, peer).wait_recv())

    def forth_step(i, carry):
        weight = plane_of(passed_all, i)
        weights = jnp.concatenate([weight] * 4, axis=0)
        fields = work[i]
        crossed = jnp.concatenate([fields[:, 128:] * weights, fields[:, :128] * weights], axis=1)
        half = product(crossed, *tables("lanes"))
        work[i] = product(turned(half), *tables("slots"))
        one_spread(plane_of(state_all, i) * weight, product_spectrum, i)
        return carry

    lax.fori_loop(0, 8, forth_step, 0)

    for residue in range(4):

        def total_step(r, carry, residue=residue):
            rows = pl.ds(pl.multiple_of(residue * 32 + r * 8, 8), 8)
            pairs = forward_eight(load_eight(work, rows), residue)
            lost = forward_eight(load_eight(product_spectrum, rows), residue)
            total = []
            for n in range(8):
                (re, im), (lost_re, lost_im) = pairs[n], lost[n]
                even_l, even_r = even_left[n, rows, :], even_right[n, rows, :]
                even_c = even_loss[n, rows, :]
                total.append(
                    (
                        even_l * re + even_r * im - even_c * lost_re,
                        even_l * im - even_r * re - even_c * lost_im,
                    )
                )
            store_eight(work, rows, backward_eight(total, residue))
            return carry

        lax.fori_loop(0, 4, total_step, 0)

    def last_step(i, carry):
        value = one_field(work[i]) - plane_of(passed_all, i) * loss_field[i]
        result[pl.ds(i, 32, stride=8), :] = value
        return carry

    lax.fori_loop(0, 8, last_step, 0)

    def result_copy(peer):
        return pltpu.make_async_remote_copy(
            src_ref=result.at[pl.ds(peer * 16, 16), :],
            dst_ref=arrived.at[quad],
            send_sem=result_send.at[peer],
            recv_sem=result_recv.at[quad],
            device_id={"quad": peer},
            device_id_type=MESH,
        )

    def result_arrival(peer):
        return pltpu.make_async_remote_copy(
            src_ref=result.at[pl.ds(peer * 16, 16), :],
            dst_ref=arrived.at[peer],
            send_sem=result_send.at[peer],
            recv_sem=result_recv.at[peer],
            device_id={"quad": peer},
            device_id_type=MESH,
        )

    for_peers(lambda peer: result_copy(peer).start())
    arrived[quad] = result[pl.ds(quad * 16, 16), :]
    for_peers(lambda peer: result_arrival(peer).wait_recv())

    for j in range(2):
        rows = slice(8 * j, 8 * j + 8)
        cells = [
            arrived[cell, rows, :]
            + arrived[4 + cell, rows, :]
            + arrived[8 + cell, rows, :]
            + arrived[12 + cell, rows, :]
            for cell in range(4)
        ]
        parts = exchange_lanes(cells)
        for h in range(4):
            part = slice(8 * h, 8 * h + 8)
            out[j, part, :] = passed_own[j, part, :] + parts[h] * (1.0 / 16.0)

    halo.wait_send()
    for_peers(lambda peer: to_peer(*state_refs, peer).wait_send())
    for_peers(lambda peer: to_peer(*passed_refs, peer).wait_send())
    for_peers(lambda peer: result_copy(peer).wait_send())
    for step in (1, 3, 2):
        position = lax.rem(column + step, 4)
        gain_copy(position).wait_send()
        gain_arrival(position, core, share_send, share_recv).wait_send()


def local(adjoint_next, saved_state, gain_left, gain_right):
    share = adjoint_next.shape
    whole_field = pltpu.VMEM((8, 128, 256), jnp.float32)
    real_spectrum = pltpu.VMEM((8, 128, 128), jnp.float32)
    dma = pltpu.SemaphoreType.DMA
    in_vmem = pl.BlockSpec(memory_space=pltpu.VMEM)
    anywhere = pl.BlockSpec(memory_space=pl.ANY)
    table = jnp.asarray(make_tables())
    return pl.pallas_call(
        kernel,
        out_shape=jax.ShapeDtypeStruct(share, jnp.float32),
        in_specs=[in_vmem, in_vmem, anywhere, anywhere, anywhere],
        out_specs=in_vmem,
        scratch_shapes=[
            pltpu.VMEM((TABLE_ROWS, 256), jnp.bfloat16),
            pltpu.VMEM(share, jnp.float32),
            pltpu.VMEM(share, jnp.float32),
            pltpu.VMEM((4, 16, 128), jnp.float32),
            pltpu.VMEM((4, 16, 128), jnp.float32),
            pltpu.VMEM((256, 128), jnp.float32),
            pltpu.VMEM((256, 128), jnp.float32),
            pltpu.VMEM((256, 128), jnp.float32),
            pltpu.VMEM((16, 16, 128), jnp.float32),
            pltpu.VMEM((2, 128, 1024), jnp.float32),
            pltpu.VMEM((4, 8, 128, 128), jnp.float32),
            real_spectrum,
            real_spectrum,
            real_spectrum,
            whole_field,
            whole_field,
            whole_field,
            whole_field,
            pltpu.VMEM((8, 32, 128), jnp.float32),
            dma((3,)),
            dma((2,)),
            dma((16,)),
            dma((16,)),
            dma((16,)),
            dma((16,)),
            dma((16,)),
            dma((16,)),
            dma((4,)),
            dma((4,)),
            dma((4,)),
            dma((4,)),
        ],
        compiler_params=pltpu.CompilerParams(
            collective_id=0, has_side_effects=True, vmem_limit_bytes=40 * 1024 * 1024
        ),
        name="adjoint_step",
    )(adjoint_next, saved_state, gain_left, gain_right, table)


def solution(mesh):
    in_specs = (
        P("quad", None, "tile"),
        P("quad", None, "tile"),
        P("quad", None, None),
        P("quad", None, None),
    )
    out_specs = P("quad", None, "tile")
    return jax.shard_map(local, mesh=mesh, in_specs=in_specs, out_specs=out_specs, check_vma=False)
```

```python
import functools
import ml_dtypes
import numpy as np
import jax
import jax.numpy as jnp
from jax import lax
from jax.experimental import pallas as pl
from jax.experimental.pallas import tpu as pltpu
from jax.sharding import PartitionSpec as P

MESH = pl.DeviceIdType.MESH
NV = 32
BLOCK = 8
FARTHEST_FIRST = sorted(
    ((over, across) for over in range(4) for across in range(4) if over or across),
    key=lambda step: -(2 * min(step[0], 4 - step[0]) + min(step[1], 4 - step[1])),
)
HALF = 640
ROOT_HALF = float(np.sqrt(0.5))


def in_real_form(matrix):
    return np.block([[matrix.real, matrix.imag], [-matrix.imag, matrix.real]])


def two_halves(matrix):
    high = matrix.astype(ml_dtypes.bfloat16)
    low = (matrix - high.astype(np.float64)).astype(ml_dtypes.bfloat16)
    return high, low


def make_tables():
    steps = np.arange(NV)
    whole = np.exp(-2j * np.pi * (steps[:, None] * steps[None, :] % NV) / NV)
    four = np.arange(4)
    quarter = np.exp(-2j * np.pi * (four[:, None] * four[None, :] % 4) / 4)
    lanes = np.kron(quarter, whole)
    slots = np.kron(np.eye(4), whole)
    blocks = [
        in_real_form(lanes),
        in_real_form(slots),
        in_real_form(np.tile(whole, (1, 4))),
        in_real_form(slots.conj() / NV),
        in_real_form(lanes.conj() / NV**2),
    ]
    rows = []
    for block in blocks:
        rows.extend(two_halves(block))
    total = in_real_form(np.tile(whole.conj() / NV, (4, 1)))
    total = np.concatenate([total, np.zeros((256, 64))], axis=1)
    rows.append(np.concatenate(two_halves(total), axis=1))
    return np.concatenate(rows, axis=0)


ROWS_OF = {
    "lanes": (0, 256, 256),
    "slots": (512, 768, 256),
    "spread": (1024, 1088, 64),
    "slots_back": (1152, 1408, 256),
    "lanes_back": (1664, 1920, 256),
}
TOTAL_ROW = 2176
TABLE_ROWS = 2432


def split(x):
    high = x.astype(jnp.bfloat16)
    low = (x - high.astype(jnp.float32)).astype(jnp.bfloat16)
    return high, low


def product(x, high, low):
    xh, xl = split(x)
    dot = functools.partial(jnp.dot, preferred_element_type=jnp.float32)
    return dot(jnp.concatenate([xh, xl, xh], axis=1), jnp.concatenate([high, high, low], axis=0))


def turned(x):
    return jnp.concatenate([x[:, :128].T, x[:, 128:].T], axis=1)


def turn_by(value, factor):
    re, im = value
    fr, fi = factor
    if abs(fi) < 1e-12 and abs(fr - 1.0) < 1e-12:
        return value
    return (re * fr - im * fi, re * fi + im * fr)


def plus(a, b):
    return (a[0] + b[0], a[1] + b[1])


def minus(a, b):
    return (a[0] - b[0], a[1] - b[1])


def four_points(x, sign):
    s0, d0 = plus(x[0], x[2]), minus(x[0], x[2])
    s1, d1 = plus(x[1], x[3]), minus(x[1], x[3])
    side = (-sign * d1[1], sign * d1[0]) if sign > 0 else (d1[1], -d1[0])
    return [plus(s0, s1), plus(d0, side), minus(s0, s1), minus(d0, side)]


def eight_points(x, sign):
    even = four_points(x[0::2], sign)
    odd = four_points(x[1::2], sign)
    o1, o2, o3 = odd[1], odd[2], odd[3]
    if sign < 0:
        o1 = ((o1[0] + o1[1]) * ROOT_HALF, (o1[1] - o1[0]) * ROOT_HALF)
        o2 = (o2[1], -o2[0])
        o3 = ((o3[1] - o3[0]) * ROOT_HALF, (o3[0] + o3[1]) * -ROOT_HALF)
    else:
        o1 = ((o1[0] - o1[1]) * ROOT_HALF, (o1[1] + o1[0]) * ROOT_HALF)
        o2 = (-o2[1], o2[0])
        o3 = ((o3[0] + o3[1]) * -ROOT_HALF, (o3[0] - o3[1]) * ROOT_HALF)
    odd = [odd[0], o1, o2, o3]
    return [plus(e, o) for e, o in zip(even, odd)] + [minus(e, o) for e, o in zip(even, odd)]


def twiddle(index, residue, sign):
    angle = sign * 2.0 * np.pi * (index * residue % NV) / NV
    return float(np.cos(angle)), float(np.sin(angle))


def forward_eight(x, residue):
    return eight_points([turn_by(v, twiddle(n, residue, -1)) for n, v in enumerate(x)], -1)


def backward_eight(x, residue):
    return [turn_by(v, twiddle(n, residue, 1)) for n, v in enumerate(eight_points(x, 1))]


def exchange_lanes(tiles):
    group = lax.broadcasted_iota(jnp.int32, (8, 128), 1) // 32
    upper = group >= 2
    odd = group % 2 == 1
    y = [None] * 4
    for h in range(2):
        y[h] = jnp.where(upper, pltpu.roll(tiles[h + 2], 64, 1), tiles[h])
        y[h + 2] = jnp.where(upper, tiles[h + 2], pltpu.roll(tiles[h], 64, 1))
    z = [None] * 4
    for h in (0, 2):
        z[h] = jnp.where(odd, pltpu.roll(y[h + 1], 32, 1), y[h])
        z[h + 1] = jnp.where(odd, y[h + 1], pltpu.roll(y[h], 96, 1))
    return z


def kernel(
    adjoint_hbm,
    state_hbm,
    gain_left,
    gain_right,
    table_hbm,
    out,
    table,
    adjoint,
    state,
    beside,
    passed_own,
    state_sent,
    passed_sent,
    state_all,
    passed_all,
    result,
    arrived,
    raw,
    gains,
    even,
    spectrum,
    product_spectrum,
    work,
    loss_work,
    local_sem,
    halo_sem,
    state_send,
    state_recv,
    passed_send,
    passed_recv,
    result_send,
    result_recv,
    gain_send,
    gain_recv,
    share_send,
    share_recv,
    loss_send,
    loss_recv,
):
    tile = lax.axis_index("tile")
    quad = lax.axis_index("quad")
    tiles = lax.axis_size("tile")
    column = lax.rem(quad, 4)
    row = quad // 4
    core = lax.rem(tile, 2)
    sibling = tile + 1 - 2 * core
    ahead = quad >= 8
    up, down = lax.rem(tile + 1, tiles), lax.rem(tile + tiles - 1, tiles)
    source_tile = jnp.where(ahead, up, down)
    target_tile = jnp.where(ahead, down, up)

    fetch_table = pltpu.make_async_copy(table_hbm, table, local_sem.at[0])
    fetch_left = pltpu.make_async_copy(gain_left.at[0], raw.at[0], local_sem.at[1])
    fetch_right = pltpu.make_async_copy(gain_right.at[0], raw.at[1], local_sem.at[2])
    fetch_state = pltpu.make_async_copy(state_hbm, state, local_sem.at[3])
    fetch_adjoint = pltpu.make_async_copy(adjoint_hbm, adjoint, local_sem.at[4])
    fetch_state.start()
    fetch_adjoint.start()
    fetch_left.start()
    fetch_right.start()
    fetch_table.start()

    barrier = pltpu.get_barrier_semaphore()

    def greet(step, carry):
        peer = lax.rem(quad + step, 16)
        pl.semaphore_signal(barrier, inc=1, device_id={"quad": peer}, device_id_type=MESH)
        return carry

    lax.fori_loop(1, 16, greet, 0)
    pl.semaphore_signal(barrier, inc=1, device_id={"tile": source_tile}, device_id_type=MESH)
    pl.semaphore_signal(barrier, inc=1, device_id={"tile": sibling}, device_id_type=MESH)

    fetch_left.wait()
    fetch_right.wait()
    lane = lax.broadcasted_iota(jnp.int32, (8, 128), 1)
    line = lax.broadcasted_iota(jnp.int32, (8, 128), 0)
    mirror_lane = lax.rem(4 - lane // 32, 4) * 32 + lax.rem(32 - lax.rem(lane, 32), 32)
    mirror_line = lax.rem(8 - line, 8)

    def mirrored_source(kind, h, r):
        def lines(t, n):
            return raw[kind, 8 * n : 8 * n + 8, 128 * t : 128 * t + 128]

        def column_mirrored(n):
            return jnp.where(lane < 32, lines((8 - h) % 8, n), lines((7 - h) % 8, n))

        first = column_mirrored((4 - r) % 4)
        rest = jnp.take_along_axis(column_mirrored(3 - r), mirror_line, axis=0)
        return jnp.where(line == 0, first, rest)

    own_rows = column * 32
    for h in range(5):
        for r in range(4):
            at = pl.ds(own_rows + 8 * r, 8)
            here = slice(128 * h, 128 * h + 128)
            left, right = (raw[kind, 8 * r : 8 * r + 8, here] for kind in range(2))
            left_m, right_m = (
                jnp.take_along_axis(source, mirror_lane, axis=1)
                for source in (mirrored_source(0, h, r), mirrored_source(1, h, r))
            )
            gains[0, at, here] = (left + left_m) * 0.5
            gains[1, at, here] = (right + right_m) * 0.5
            gains[2, at, here] = (left * right + left_m * right_m) * 0.5

    fetch_state.wait()
    for j in range(2):
        cells = exchange_lanes([state[j, 8 * h : 8 * h + 8, :] for h in range(4)])
        for cell in range(4):
            state_sent[cell, 8 * j : 8 * j + 8, :] = cells[cell]
    state_all[pl.ds(quad * 16, 16), :] = state_sent[column]

    pl.semaphore_wait(barrier, 17)

    halo = pltpu.make_async_remote_copy(
        src_ref=adjoint,
        dst_ref=beside,
        send_sem=halo_sem.at[0],
        recv_sem=halo_sem.at[1],
        device_id={"tile": target_tile},
        device_id_type=MESH,
    )
    fetch_adjoint.wait()
    halo.start()

    def to_peer(sent, whole, send, recv, peer):
        return pltpu.make_async_remote_copy(
            src_ref=sent.at[lax.rem(peer, 4)],
            dst_ref=whole.at[pl.ds(quad * 16, 16), :],
            send_sem=send.at[peer],
            recv_sem=recv.at[quad],
            device_id={"quad": peer},
            device_id_type=MESH,
        )

    def from_peer(sent, whole, send, recv, peer):
        return pltpu.make_async_remote_copy(
            src_ref=sent.at[0],
            dst_ref=whole.at[pl.ds(peer * 16, 16), :],
            send_sem=send.at[peer],
            recv_sem=recv.at[peer],
            device_id={"quad": peer},
            device_id_type=MESH,
        )

    def for_peers(action):
        for over, across in FARTHEST_FIRST:
            action(lax.rem(row + over, 4) * 4 + lax.rem(column + across, 4))

    state_refs = (state_sent, state_all, state_send, state_recv)
    passed_refs = (passed_sent, passed_all, passed_send, passed_recv)

    def gain_copy(kind, send, recv, position):
        return pltpu.make_async_remote_copy(
            src_ref=gains.at[kind, pl.ds(column * 32, 32), :],
            dst_ref=gains.at[kind, pl.ds(column * 32, 32), :],
            send_sem=send.at[position],
            recv_sem=recv.at[column],
            device_id={"quad": row * 4 + position},
            device_id_type=MESH,
        )

    def gain_arrival(position, kind, send, recv):
        return pltpu.make_async_remote_copy(
            src_ref=gains.at[kind, pl.ds(position * 32, 32), :],
            dst_ref=gains.at[kind, pl.ds(position * 32, 32), :],
            send_sem=send.at[position],
            recv_sem=recv.at[position],
            device_id={"tile": sibling},
            device_id_type=MESH,
        )

    beside_columns = [lax.rem(column + step, 4) for step in (2, 1, 3)]
    for position in beside_columns:
        gain_copy(core, gain_send, gain_recv, position).start()
    for_peers(lambda peer: to_peer(*state_refs, peer).start())

    halo.wait_recv()
    lower = lane < 64
    odd_cell = lane // 32 % 2 == 1
    from_own = jnp.logical_xor(lower, jnp.logical_not(ahead))
    for j in range(2):
        plane = (quad * 2 + j).astype(jnp.float32)
        speed_x = jnp.abs((plane - (NV - 1) / 2.0) / NV)
        for h in range(4):
            rows = slice(8 * h, 8 * h + 8)
            own = adjoint[j, rows, :]
            second = beside[j, rows, :]
            first = jnp.where(from_own, pltpu.roll(own, 64, 1), pltpu.roll(second, 64, 1))
            partner = jnp.where(odd_cell, pltpu.roll(own, 32, 1), pltpu.roll(own, 96, 1))
            b = (lax.broadcasted_iota(jnp.int32, (8, 128), 0) + 8 * h).astype(jnp.float32)
            speed_y = jnp.abs((b - (NV - 1) / 2.0) / NV)
            passed_own[j, rows, :] = (
                own
                - speed_x * (3.0 * own - 4.0 * first + second) * 0.5
                - 2.0 * speed_y * (own - partner)
            )
        cells = exchange_lanes([passed_own[j, 8 * h : 8 * h + 8, :] for h in range(4)])
        for cell in range(4):
            passed_sent[cell, 8 * j : 8 * j + 8, :] = cells[cell]
    passed_all[pl.ds(quad * 16, 16), :] = passed_sent[column]
    for_peers(lambda peer: to_peer(*passed_refs, peer).start())
    for position in beside_columns:
        gain_copy(2, loss_send, loss_recv, position).start()

    def tables(name):
        high, low, count = ROWS_OF[name]
        return table[high : high + count, :], table[low : low + count, :]

    def spread(values):
        high, low = tables("lanes")
        mid = product(values, high[:128], low[:128])
        parts = [mid[n : n + 32] for n in range(0, values.shape[0], 32)]
        parts = [jnp.concatenate([part[:, :128], part[:, 128:]], axis=0).T for part in parts]
        return product(jnp.concatenate(parts, axis=0), *tables("spread"))

    def plane_of(ref, low_index):
        return ref[pl.ds(low_index, 32, stride=8), :]

    fetch_table.wait()
    for_peers(lambda peer: from_peer(*state_refs, peer).wait_recv())

    for i in range(0, 8, BLOCK):
        planes = jnp.concatenate([plane_of(state_all, i + n) for n in range(BLOCK)], axis=0)
        spectrum[i : i + BLOCK] = spread(planes).reshape(BLOCK, 128, 256)

    def load_eight(ref, rows):
        return [(ref[n, rows, :128], ref[n, rows, 128:]) for n in range(8)]

    def store_eight(ref, rows, values):
        for n, (re, im) in enumerate(values):
            ref[n, rows, :128] = re
            ref[n, rows, 128:] = im

    def over_rows(step):
        for residue in range(4):

            def body(r, carry, residue=residue):
                step(residue, pl.ds(pl.multiple_of(residue * 32 + r * 8, 8), 8))
                return carry

            lax.fori_loop(0, 4, body, 0)

    def finish_forward(ref):
        def step(residue, rows):
            store_eight(ref, rows, forward_eight(load_eight(ref, rows), residue))

        over_rows(step)

    finish_forward(spectrum)

    lanes = lax.broadcasted_iota(jnp.int32, (128, 128), 1)
    mirror_low = lax.rem(4 - lanes // 32, 4) * 32 + lax.rem(32 - lax.rem(lanes, 32), 32)
    mirror_one = lanes // 32 * 32 + lax.rem(32 - lax.rem(lanes, 32), 32)

    def unfold(kind):
        for h in range(5):
            block = gains[kind, :, 128 * h : 128 * h + 128]
            if h == 4:
                even[kind, 4, :32, :] = block.T[:32]
                continue
            even[kind, h] = block.T
            other = jnp.take_along_axis(block, mirror_low, axis=1).T
            other = jnp.take_along_axis(other, mirror_one, axis=1)
            even[kind, 7 - h, 32:, :] = other[32:]
            if h:
                even[kind, 8 - h, :32, :] = other[:32]

    for position in beside_columns:
        gain_arrival(position, core, gain_send, gain_recv).wait_recv()
        gain_arrival(position, core, share_send, share_recv).start()
    unfold(core)

    for_peers(lambda peer: from_peer(*passed_refs, peer).wait_recv())
    for i in range(0, 8, BLOCK):
        planes = [plane_of(state_all, n) * plane_of(passed_all, n) for n in range(i, i + BLOCK)]
        fields = spread(jnp.concatenate(planes, axis=0))
        product_spectrum[i : i + BLOCK] = fields.reshape(BLOCK, 128, 256)
    finish_forward(product_spectrum)

    for position in beside_columns:
        gain_arrival(position, 1 - core, share_send, share_recv).wait_recv()
    unfold(1 - core)

    def filter_step(residue, rows):
        both = []
        for n, (re, im) in enumerate(load_eight(spectrum, rows)):
            left, right = even[0, n, rows, :], even[1, n, rows, :]
            both.append((left * re - right * im, left * im + right * re))
        store_eight(work, rows, backward_eight(both, residue))

    over_rows(filter_step)

    def summed_fields(values):
        half = product(
            values,
            table[TOTAL_ROW : TOTAL_ROW + 256, :128],
            table[TOTAL_ROW : TOTAL_ROW + 256, 128:],
        )
        parts = [half[n : n + 128].T for n in range(0, values.shape[0], 128)]
        parts = [jnp.concatenate([part[:32], part[32:64]], axis=1) for part in parts]
        high, low = tables("lanes_back")
        return product(jnp.concatenate(parts, axis=0), high[:, :128], low[:, :128])

    def all_turned(values):
        parts = [turned(values[n : n + 128]) for n in range(0, values.shape[0], 128)]
        return jnp.concatenate(parts, axis=0)

    for i in range(0, 8, BLOCK):
        half = product(work[i : i + BLOCK].reshape(BLOCK * 128, 256), *tables("slots_back"))
        fields = product(all_turned(half), *tables("lanes_back"))
        work[i : i + BLOCK] = fields.reshape(BLOCK, 128, 256)
    for i in range(0, 8, BLOCK):
        crossed = []
        for n in range(i, i + BLOCK):
            weights = jnp.concatenate([plane_of(passed_all, n)] * 4, axis=0)
            fields = work[n]
            crossed.append(
                jnp.concatenate([fields[:, 128:] * weights, fields[:, :128] * weights], axis=1)
            )
        half = product(jnp.concatenate(crossed, axis=0), *tables("lanes"))
        fields = product(all_turned(half), *tables("slots"))
        work[i : i + BLOCK] = fields.reshape(BLOCK, 128, 256)
    for position in beside_columns:
        gain_arrival(position, 2, loss_send, loss_recv).wait_recv()
    unfold(2)

    def total_step(residue, rows):
        pairs = forward_eight(load_eight(work, rows), residue)
        lost = load_eight(product_spectrum, rows)
        whole = load_eight(spectrum, rows)
        total, loss = [], []
        for n in range(8):
            (re, im), (lost_re, lost_im) = pairs[n], lost[n]
            left, right, both = (even[kind, n, rows, :] for kind in range(3))
            total.append(
                (left * re + right * im - both * lost_re, left * im - right * re - both * lost_im)
            )
            loss.append((both * whole[n][0], both * whole[n][1]))
        store_eight(work, rows, backward_eight(total, residue))
        store_eight(loss_work, rows, backward_eight(loss, residue))

    over_rows(total_step)

    for i in range(0, 8, BLOCK):
        fields = summed_fields(work[i : i + BLOCK].reshape(BLOCK * 128, 256))
        losses = summed_fields(loss_work[i : i + BLOCK].reshape(BLOCK * 128, 256))
        for n in range(BLOCK):
            own = slice(32 * n, 32 * n + 32)
            value = fields[own] - plane_of(passed_all, i + n) * losses[own]
            result[pl.ds(i + n, 32, stride=8), :] = value

    def result_copy(peer):
        return pltpu.make_async_remote_copy(
            src_ref=result.at[pl.ds(peer * 16, 16), :],
            dst_ref=arrived.at[quad],
            send_sem=result_send.at[peer],
            recv_sem=result_recv.at[quad],
            device_id={"quad": peer},
            device_id_type=MESH,
        )

    def result_arrival(peer):
        return pltpu.make_async_remote_copy(
            src_ref=result.at[pl.ds(peer * 16, 16), :],
            dst_ref=arrived.at[peer],
            send_sem=result_send.at[peer],
            recv_sem=result_recv.at[peer],
            device_id={"quad": peer},
            device_id_type=MESH,
        )

    for_peers(lambda peer: result_copy(peer).start())
    arrived[quad] = result[pl.ds(quad * 16, 16), :]
    for_peers(lambda peer: result_arrival(peer).wait_recv())

    for j in range(2):
        rows = slice(8 * j, 8 * j + 8)
        cells = [
            arrived[cell, rows, :]
            + arrived[4 + cell, rows, :]
            + arrived[8 + cell, rows, :]
            + arrived[12 + cell, rows, :]
            for cell in range(4)
        ]
        parts = exchange_lanes(cells)
        for h in range(4):
            part = slice(8 * h, 8 * h + 8)
            out[j, part, :] = passed_own[j, part, :] + parts[h] * (1.0 / 16.0)

    halo.wait_send()
    for_peers(lambda peer: to_peer(*state_refs, peer).wait_send())
    for_peers(lambda peer: to_peer(*passed_refs, peer).wait_send())
    for_peers(lambda peer: result_copy(peer).wait_send())
    for position in beside_columns:
        gain_copy(core, gain_send, gain_recv, position).wait_send()
        gain_copy(2, loss_send, loss_recv, position).wait_send()
        gain_arrival(position, core, share_send, share_recv).wait_send()


def local(adjoint_next, saved_state, gain_left, gain_right):
    share = adjoint_next.shape
    whole_field = pltpu.VMEM((8, 128, 256), jnp.float32)
    dma = pltpu.SemaphoreType.DMA
    in_vmem = pl.BlockSpec(memory_space=pltpu.VMEM)
    anywhere = pl.BlockSpec(memory_space=pl.ANY)
    table = jnp.asarray(make_tables())
    return pl.pallas_call(
        kernel,
        out_shape=jax.ShapeDtypeStruct(share, jnp.float32),
        in_specs=[anywhere] * 5,
        out_specs=in_vmem,
        scratch_shapes=[
            pltpu.VMEM((TABLE_ROWS, 256), jnp.bfloat16),
            pltpu.VMEM(share, jnp.float32),
            pltpu.VMEM(share, jnp.float32),
            pltpu.VMEM(share, jnp.float32),
            pltpu.VMEM(share, jnp.float32),
            pltpu.VMEM((4, 16, 128), jnp.float32),
            pltpu.VMEM((4, 16, 128), jnp.float32),
            pltpu.VMEM((256, 128), jnp.float32),
            pltpu.VMEM((256, 128), jnp.float32),
            pltpu.VMEM((256, 128), jnp.float32),
            pltpu.VMEM((16, 16, 128), jnp.float32),
            pltpu.VMEM((2, NV, 1024), jnp.float32),
            pltpu.VMEM((3, 128, HALF), jnp.float32),
            pltpu.VMEM((3, 8, 128, 128), jnp.float32),
            whole_field,
            whole_field,
            whole_field,
            whole_field,
            dma((5,)),
            dma((2,)),
            dma((16,)),
            dma((16,)),
            dma((16,)),
            dma((16,)),
            dma((16,)),
            dma((16,)),
            dma((4,)),
            dma((4,)),
            dma((4,)),
            dma((4,)),
            dma((4,)),
            dma((4,)),
        ],
        compiler_params=pltpu.CompilerParams(
            collective_id=0, has_side_effects=True, vmem_limit_bytes=60 * 1024 * 1024
        ),
        name="adjoint_step",
    )(adjoint_next, saved_state, gain_left, gain_right, table)


def solution(mesh):
    in_specs = (
        P("quad", None, "tile"),
        P("quad", None, "tile"),
        P("quad", None, None),
        P("quad", None, None),
    )
    out_specs = P("quad", None, "tile")
    return jax.shard_map(local, mesh=mesh, in_specs=in_specs, out_specs=out_specs, check_vma=False)
```

```python
import functools
import ml_dtypes
import numpy as np
import jax
import jax.numpy as jnp
from jax import lax
from jax.experimental import pallas as pl
from jax.experimental.pallas import tpu as pltpu
from jax.sharding import PartitionSpec as P

MESH = pl.DeviceIdType.MESH
NV = 32
BLOCK = 8
FARTHEST_FIRST = sorted(
    ((over, across) for over in range(4) for across in range(4) if over or across),
    key=lambda step: -(2 * min(step[0], 4 - step[0]) + min(step[1], 4 - step[1])),
)
HALF = 640
ROOT_HALF = float(np.sqrt(0.5))


def in_real_form(matrix):
    return np.block([[matrix.real, matrix.imag], [-matrix.imag, matrix.real]])


def two_halves(matrix):
    high = matrix.astype(ml_dtypes.bfloat16)
    low = (matrix - high.astype(np.float64)).astype(ml_dtypes.bfloat16)
    return high, low


def make_tables():
    steps = np.arange(NV)
    whole = np.exp(-2j * np.pi * (steps[:, None] * steps[None, :] % NV) / NV)
    four = np.arange(4)
    quarter = np.exp(-2j * np.pi * (four[:, None] * four[None, :] % 4) / 4)
    lanes = np.kron(quarter, whole)
    slots = np.kron(np.eye(4), whole)
    blocks = [
        in_real_form(lanes),
        in_real_form(slots),
        in_real_form(slots.conj() / NV),
        in_real_form(lanes.conj() / NV**2),
    ]
    rows = []
    for block in blocks:
        rows.extend(two_halves(block))
    back = whole.conj() / NV
    for left in (
        np.concatenate([whole.real, whole.imag], axis=0),
        np.concatenate([back.real, -back.imag], axis=1),
    ):
        high, low = two_halves(left)
        wide = np.concatenate([high, high, low], axis=1)
        rows.append(np.pad(wide, ((0, 0), (0, 256 - wide.shape[1]))))
    return np.concatenate(rows, axis=0)


def make_twiddles():
    angle = -2.0 * np.pi * (np.arange(8)[:, None] * (np.arange(128)[None, :] // 32)) / NV
    parts = np.stack([np.cos(angle), np.sin(angle)], axis=1).astype(np.float32)
    return np.broadcast_to(parts[:, :, None, :], (8, 2, 8, 128)).reshape(128, 128).copy()


ROWS_OF = {
    "lanes": (0, 256),
    "slots": (512, 768),
    "slots_back": (1024, 1280),
    "lanes_back": (1536, 1792),
}
LEFT_ROW = 2048
LEFT_BACK_ROW = 2112
TABLE_ROWS = 2144


def split(x):
    high = x.astype(jnp.bfloat16)
    low = (x - high.astype(jnp.float32)).astype(jnp.bfloat16)
    return high, low


def dot(a, b):
    return jnp.dot(a, b, preferred_element_type=jnp.float32)


def product(x, high, low):
    xh, xl = split(x)
    return dot(
        jnp.concatenate([xh, xl, xh], axis=1), jnp.concatenate([high, high, low], axis=0)
    )


def left_product(left, x):
    xh, xl = split(x)
    return dot(left, jnp.concatenate([xh, xl, xh], axis=0))


def turned(x):
    return jnp.concatenate([x[:, :128].T, x[:, 128:].T], axis=1)


def turn_by(value, factor):
    re, im = value
    fr, fi = factor
    return (re * fr - im * fi, re * fi + im * fr)


def plus(a, b):
    return (a[0] + b[0], a[1] + b[1])


def minus(a, b):
    return (a[0] - b[0], a[1] - b[1])


def four_points(x, sign):
    s0, d0 = plus(x[0], x[2]), minus(x[0], x[2])
    s1, d1 = plus(x[1], x[3]), minus(x[1], x[3])
    side = (-sign * d1[1], sign * d1[0]) if sign > 0 else (d1[1], -d1[0])
    return [plus(s0, s1), plus(d0, side), minus(s0, s1), minus(d0, side)]


def eight_points(x, sign):
    even = four_points(x[0::2], sign)
    odd = four_points(x[1::2], sign)
    o1, o2, o3 = odd[1], odd[2], odd[3]
    if sign < 0:
        o1 = ((o1[0] + o1[1]) * ROOT_HALF, (o1[1] - o1[0]) * ROOT_HALF)
        o2 = (o2[1], -o2[0])
        o3 = ((o3[1] - o3[0]) * ROOT_HALF, (o3[0] + o3[1]) * -ROOT_HALF)
    else:
        o1 = ((o1[0] - o1[1]) * ROOT_HALF, (o1[1] + o1[0]) * ROOT_HALF)
        o2 = (-o2[1], o2[0])
        o3 = ((o3[0] + o3[1]) * -ROOT_HALF, (o3[0] - o3[1]) * ROOT_HALF)
    odd = [odd[0], o1, o2, o3]
    return [plus(e, o) for e, o in zip(even, odd)] + [minus(e, o) for e, o in zip(even, odd)]


def forward_eight(x, factors):
    turned_x = [x[0]] + [turn_by(v, f) for v, f in zip(x[1:], factors)]
    return eight_points(turned_x, -1)


def backward_eight(x, factors):
    y = eight_points(x, 1)
    return [y[0]] + [turn_by(v, (fr, -fi)) for v, (fr, fi) in zip(y[1:], factors)]


def exchange_lanes(tiles):
    group = lax.broadcasted_iota(jnp.int32, (8, 128), 1) // 32
    upper = group >= 2
    odd = group % 2 == 1
    y = [None] * 4
    for h in range(2):
        y[h] = jnp.where(upper, pltpu.roll(tiles[h + 2], 64, 1), tiles[h])
        y[h + 2] = jnp.where(upper, tiles[h + 2], pltpu.roll(tiles[h], 64, 1))
    z = [None] * 4
    for h in (0, 2):
        z[h] = jnp.where(odd, pltpu.roll(y[h + 1], 32, 1), y[h])
        z[h + 1] = jnp.where(odd, y[h + 1], pltpu.roll(y[h], 96, 1))
    return z


def kernel(
    adjoint_hbm,
    state_hbm,
    gain_left,
    gain_right,
    table_hbm,
    twiddle_hbm,
    out,
    table,
    twiddles,
    adjoint,
    state,
    beside,
    passed_own,
    state_sent,
    passed_sent,
    state_all,
    passed_all,
    result,
    arrived,
    raw,
    gains,
    upper,
    loss_gain,
    loss_upper,
    spectrum,
    product_spectrum,
    total,
    loss,
    work,
    local_sem,
    halo_sem,
    state_send,
    state_recv,
    passed_send,
    passed_recv,
    result_send,
    result_recv,
    gain_send,
    gain_recv,
    share_send,
    share_recv,
    loss_send,
    loss_recv,
):
    tile = lax.axis_index("tile")
    quad = lax.axis_index("quad")
    tiles = lax.axis_size("tile")
    column = lax.rem(quad, 4)
    row = quad // 4
    core = lax.rem(tile, 2)
    sibling = tile + 1 - 2 * core
    ahead = quad >= 8
    up, down = lax.rem(tile + 1, tiles), lax.rem(tile + tiles - 1, tiles)
    source_tile = jnp.where(ahead, up, down)
    target_tile = jnp.where(ahead, down, up)

    fetch_twiddles = pltpu.make_async_copy(twiddle_hbm, twiddles, local_sem.at[5])
    fetch_table = pltpu.make_async_copy(table_hbm, table, local_sem.at[0])
    fetch_left = pltpu.make_async_copy(gain_left.at[0], raw.at[0], local_sem.at[1])
    fetch_right = pltpu.make_async_copy(gain_right.at[0], raw.at[1], local_sem.at[2])
    fetch_state = pltpu.make_async_copy(state_hbm, state, local_sem.at[3])
    fetch_adjoint = pltpu.make_async_copy(adjoint_hbm, adjoint, local_sem.at[4])
    fetch_state.start()
    fetch_adjoint.start()
    fetch_left.start()
    fetch_right.start()
    fetch_table.start()
    fetch_twiddles.start()

    barrier = pltpu.get_barrier_semaphore()

    def greet(step, carry):
        peer = lax.rem(quad + step, 16)
        pl.semaphore_signal(barrier, inc=1, device_id={"quad": peer}, device_id_type=MESH)
        return carry

    lax.fori_loop(1, 16, greet, 0)
    pl.semaphore_signal(barrier, inc=1, device_id={"tile": source_tile}, device_id_type=MESH)
    pl.semaphore_signal(barrier, inc=1, device_id={"tile": sibling}, device_id_type=MESH)

    fetch_left.wait()
    fetch_right.wait()
    lane = lax.broadcasted_iota(jnp.int32, (8, 128), 1)
    line = lax.broadcasted_iota(jnp.int32, (8, 128), 0)
    mirror_lane = lax.rem(4 - lane // 32, 4) * 32 + lax.rem(32 - lax.rem(lane, 32), 32)
    mirror_line = lax.rem(8 - line, 8)

    def mirrored(tile_of, h, r):
        def column(n):
            return jnp.where(lane < 32, tile_of((8 - h) % 8, n), tile_of((7 - h) % 8, n))

        rest = jnp.take_along_axis(column(3 - r), mirror_line, axis=0)
        both = jnp.where(line == 0, column((4 - r) % 4), rest)
        return jnp.take_along_axis(both, mirror_lane, axis=1)

    def raw_tile(kind):
        return lambda h, r: raw[kind, 8 * r : 8 * r + 8, 128 * h : 128 * h + 128]

    own_rows = column * 32
    for h in range(5):
        for r in range(4):
            at = pl.ds(own_rows + 8 * r, 8)
            here = slice(128 * h, 128 * h + 128)
            left, right = raw_tile(0)(h, r), raw_tile(1)(h, r)
            left_m, right_m = mirrored(raw_tile(0), h, r), mirrored(raw_tile(1), h, r)
            gains[0, at, here] = (left + left_m) * 0.5
            gains[1, at, here] = (right + right_m) * 0.5
            gains[2, at, here] = (left * right + left_m * right_m) * 0.5

    fetch_state.wait()
    for j in range(2):
        cells = exchange_lanes([state[j, 8 * h : 8 * h + 8, :] for h in range(4)])
        for cell in range(4):
            state_sent[cell, 8 * j : 8 * j + 8, :] = cells[cell]
    state_all[pl.ds(quad * 16, 16), :] = state_sent[column]

    pl.semaphore_wait(barrier, 17)

    halo = pltpu.make_async_remote_copy(
        src_ref=adjoint,
        dst_ref=beside,
        send_sem=halo_sem.at[0],
        recv_sem=halo_sem.at[1],
        device_id={"tile": target_tile},
        device_id_type=MESH,
    )
    fetch_adjoint.wait()
    halo.start()

    def to_peer(sent, whole, send, recv, peer):
        return pltpu.make_async_remote_copy(
            src_ref=sent.at[lax.rem(peer, 4)],
            dst_ref=whole.at[pl.ds(quad * 16, 16), :],
            send_sem=send.at[peer],
            recv_sem=recv.at[quad],
            device_id={"quad": peer},
            device_id_type=MESH,
        )

    def from_peer(sent, whole, send, recv, peer):
        return pltpu.make_async_remote_copy(
            src_ref=sent.at[0],
            dst_ref=whole.at[pl.ds(peer * 16, 16), :],
            send_sem=send.at[peer],
            recv_sem=recv.at[peer],
            device_id={"quad": peer},
            device_id_type=MESH,
        )

    def for_peers(action):
        for over, across in FARTHEST_FIRST:
            action(lax.rem(row + over, 4) * 4 + lax.rem(column + across, 4))

    state_refs = (state_sent, state_all, state_send, state_recv)
    passed_refs = (passed_sent, passed_all, passed_send, passed_recv)

    def gain_copy(kind, send, recv, position):
        return pltpu.make_async_remote_copy(
            src_ref=gains.at[kind, pl.ds(column * 32, 32), :],
            dst_ref=gains.at[kind, pl.ds(column * 32, 32), :],
            send_sem=send.at[position],
            recv_sem=recv.at[column],
            device_id={"quad": row * 4 + position},
            device_id_type=MESH,
        )

    def gain_arrival(position, kind, send, recv):
        return pltpu.make_async_remote_copy(
            src_ref=gains.at[kind, pl.ds(position * 32, 32), :],
            dst_ref=gains.at[kind, pl.ds(position * 32, 32), :],
            send_sem=send.at[position],
            recv_sem=recv.at[position],
            device_id={"tile": sibling},
            device_id_type=MESH,
        )

    beside_columns = [lax.rem(column + step, 4) for step in (2, 1, 3)]
    for position in beside_columns:
        gain_copy(core, gain_send, gain_recv, position).start()
    for_peers(lambda peer: to_peer(*state_refs, peer).start())

    halo.wait_recv()
    lower = lane < 64
    odd_cell = lane // 32 % 2 == 1
    from_own = jnp.logical_xor(lower, jnp.logical_not(ahead))
    for j in range(2):
        plane = (quad * 2 + j).astype(jnp.float32)
        speed_x = jnp.abs((plane - (NV - 1) / 2.0) / NV)
        for h in range(4):
            rows = slice(8 * h, 8 * h + 8)
            own = adjoint[j, rows, :]
            second = beside[j, rows, :]
            first = jnp.where(from_own, pltpu.roll(own, 64, 1), pltpu.roll(second, 64, 1))
            partner = jnp.where(odd_cell, pltpu.roll(own, 32, 1), pltpu.roll(own, 96, 1))
            b = (lax.broadcasted_iota(jnp.int32, (8, 128), 0) + 8 * h).astype(jnp.float32)
            speed_y = jnp.abs((b - (NV - 1) / 2.0) / NV)
            passed_own[j, rows, :] = (
                own
                - speed_x * (3.0 * own - 4.0 * first + second) * 0.5
                - 2.0 * speed_y * (own - partner)
            )
        cells = exchange_lanes([passed_own[j, 8 * h : 8 * h + 8, :] for h in range(4)])
        for cell in range(4):
            passed_sent[cell, 8 * j : 8 * j + 8, :] = cells[cell]
    passed_all[pl.ds(quad * 16, 16), :] = passed_sent[column]
    for_peers(lambda peer: to_peer(*passed_refs, peer).start())
    for position in beside_columns:
        gain_copy(2, loss_send, loss_recv, position).start()

    def tables(name):
        high, low = ROWS_OF[name]
        return table[high : high + 256, :], table[low : low + 256, :]

    def plane_of(ref, low_index):
        return ref[pl.ds(low_index, 32, stride=8), :]

    def tile_at(n):
        return slice(128 * n, 128 * n + 128)

    def factors():
        at = [slice(8 * n, 8 * n + 8) for n in range(16)]
        return [(twiddles[at[2 * n], :], twiddles[at[2 * n + 1], :]) for n in range(1, 8)]

    def load_eight(ref, rows):
        return [(ref[n, rows, :128], ref[n, rows, 128:]) for n in range(8)]

    def store_eight(ref, rows, values):
        for n, (re, im) in enumerate(values):
            ref[n, rows, :128] = re
            ref[n, rows, 128:] = im

    def eight_rows(start):
        return pl.ds(pl.multiple_of(start, 8), 8)

    def transform(planes, ref):
        left = table[LEFT_ROW : LEFT_ROW + 64, :96]
        mid = left_product(left, jnp.concatenate(planes, axis=1))
        rows = [
            jnp.concatenate([mid[:32, tile_at(n)], mid[32:, tile_at(n)]], axis=1) for n in range(8)
        ]
        ref[...] = product(jnp.concatenate(rows, axis=0), *tables("lanes")).reshape(8, NV, 256)

        def finish(r, carry):
            rows = eight_rows(8 * r)
            store_eight(ref, rows, forward_eight(load_eight(ref, rows), factors()))
            return carry

        lax.fori_loop(0, 4, finish, 0)

    fetch_table.wait()
    fetch_twiddles.wait()
    for_peers(lambda peer: from_peer(*state_refs, peer).wait_recv())
    transform([plane_of(state_all, n) for n in range(8)], spectrum)

    def unfold(kind):
        def body(pair, carry):
            def tile_of(h, r):
                return gains[kind, eight_rows(pair * 32 + 8 * r), tile_at(h)]

            for h in (7, 6, 5, 4):
                for r in range(4):
                    values = mirrored(tile_of, h, r)
                    if h == 4:
                        values = jnp.where(lane < 32, tile_of(4, r), values)
                    upper[kind, eight_rows(pair * 32 + 8 * r), tile_at(h - 4)] = values
            return carry

        lax.fori_loop(0, 4, body, 0)

    for position in beside_columns:
        gain_arrival(position, core, gain_send, gain_recv).wait_recv()
        gain_arrival(position, core, share_send, share_recv).start()
    unfold(core)

    def wait_passed():
        for_peers(lambda peer: from_peer(*passed_refs, peer).wait_recv())

    def transform_product():
        planes = [plane_of(state_all, n) * plane_of(passed_all, n) for n in range(8)]
        transform(planes, product_spectrum)

    for position in beside_columns:
        gain_arrival(position, 1 - core, share_send, share_recv).wait_recv()
    unfold(1 - core)

    def gain_tile(kind, rows, n):
        return gains[kind, rows, tile_at(n)] if n < 4 else upper[kind, rows, tile_at(n - 4)]

    def filter_step(r, carry):
        rows = eight_rows(8 * r)
        both = []
        for n, (re, im) in enumerate(load_eight(spectrum, eight_rows(8 * lax.rem(r, 4)))):
            left, right = gain_tile(0, rows, n), gain_tile(1, rows, n)
            both.append((left * re - right * im, left * im + right * re))
        store_eight(work, rows, backward_eight(both, factors()))
        return carry

    lax.fori_loop(0, 16, filter_step, 0)

    def all_turned(values):
        parts = [turned(values[tile_at(n)]) for n in range(values.shape[0] // 128)]
        return jnp.concatenate(parts, axis=0)

    for i in range(0, 8, BLOCK):
        half = product(work[i : i + BLOCK].reshape(BLOCK * 128, 256), *tables("lanes_back"))
        fields = product(all_turned(half), *tables("slots_back"))
        work[i : i + BLOCK] = fields.reshape(BLOCK, 128, 256)

    wait_passed()
    for i in range(0, 8, BLOCK):
        crossed = []
        for n in range(i, i + BLOCK):
            weights = jnp.concatenate([plane_of(passed_all, n)] * 4, axis=0).T
            fields = work[n]
            crossed.append(
                jnp.concatenate([fields[:, 128:] * weights, fields[:, :128] * weights], axis=1)
            )
        half = product(jnp.concatenate(crossed, axis=0), *tables("slots"))
        fields = product(all_turned(half), *tables("lanes"))
        work[i : i + BLOCK] = fields.reshape(BLOCK, 128, 256)
    transform_product()

    for position in beside_columns:
        gain_arrival(position, 2, loss_send, loss_recv).wait_recv()

    def loss_tile(h, r):
        return loss_gain[8 * r : 8 * r + 8, tile_at(h)]

    for r in range(4):
        for h in range(5):
            starts = [32 * pair + 8 * r for pair in range(4)]
            b = [gains[2, start : start + 8, tile_at(h)] for start in starts]
            loss_gain[8 * r : 8 * r + 8, tile_at(h)] = (b[0] + b[1]) + (b[2] + b[3])
    for h in (7, 6, 5, 4):
        for r in range(4):
            values = mirrored(loss_tile, h, r)
            if h == 4:
                values = jnp.where(lane < 32, loss_tile(4, r), values)
            loss_upper[8 * r : 8 * r + 8, tile_at(h - 4)] = values

    def total_step(r, carry):
        rows = eight_rows(8 * r)
        sums = []
        weights = [loss_gain[rows, tile_at(n)] for n in range(4)]
        weights += [loss_upper[rows, tile_at(n)] for n in range(4)]
        for n, (re, im) in enumerate(load_eight(product_spectrum, rows)):
            sums.append((-weights[n] * re, -weights[n] * im))
        for pair in range(4):
            at = eight_rows(32 * pair + 8 * r)
            for n, (re, im) in enumerate(forward_eight(load_eight(work, at), factors())):
                left, right = gain_tile(0, at, n), gain_tile(1, at, n)
                sums[n] = (
                    sums[n][0] + (left * re + right * im),
                    sums[n][1] + (left * im - right * re),
                )
        store_eight(total, rows, backward_eight(sums, factors()))
        lost = [
            (weights[n] * re, weights[n] * im)
            for n, (re, im) in enumerate(load_eight(spectrum, rows))
        ]
        store_eight(loss, rows, backward_eight(lost, factors()))
        return carry

    lax.fori_loop(0, 4, total_step, 0)

    both = jnp.concatenate([total[...].reshape(256, 256), loss[...].reshape(256, 256)], axis=0)
    both = product(both, *tables("lanes_back"))

    def last_axis(values):
        parts = [values[32 * n : 32 * n + 32] for n in range(8)]
        re = jnp.concatenate([part[:, :128] for part in parts], axis=1)
        im = jnp.concatenate([part[:, 128:] for part in parts], axis=1)
        left = table[LEFT_BACK_ROW : LEFT_BACK_ROW + 32, :192]
        return left_product(left, jnp.concatenate([re, im], axis=0))

    gained, lost = last_axis(both[:256]), last_axis(both[256:])
    for n in range(8):
        value = gained[:, tile_at(n)] - plane_of(passed_all, n) * lost[:, tile_at(n)]
        result[pl.ds(n, 32, stride=8), :] = value

    def result_copy(peer):
        return pltpu.make_async_remote_copy(
            src_ref=result.at[pl.ds(peer * 16, 16), :],
            dst_ref=arrived.at[quad],
            send_sem=result_send.at[peer],
            recv_sem=result_recv.at[quad],
            device_id={"quad": peer},
            device_id_type=MESH,
        )

    def result_arrival(peer):
        return pltpu.make_async_remote_copy(
            src_ref=result.at[pl.ds(peer * 16, 16), :],
            dst_ref=arrived.at[peer],
            send_sem=result_send.at[peer],
            recv_sem=result_recv.at[peer],
            device_id={"quad": peer},
            device_id_type=MESH,
        )

    for_peers(lambda peer: result_copy(peer).start())
    arrived[quad] = result[pl.ds(quad * 16, 16), :]
    for_peers(lambda peer: result_arrival(peer).wait_recv())

    for j in range(2):
        rows = slice(8 * j, 8 * j + 8)
        cells = [
            arrived[cell, rows, :]
            + arrived[4 + cell, rows, :]
            + arrived[8 + cell, rows, :]
            + arrived[12 + cell, rows, :]
            for cell in range(4)
        ]
        parts = exchange_lanes(cells)
        for h in range(4):
            part = slice(8 * h, 8 * h + 8)
            out[j, part, :] = passed_own[j, part, :] + parts[h] * (1.0 / 16.0)

    halo.wait_send()
    for_peers(lambda peer: to_peer(*state_refs, peer).wait_send())
    for_peers(lambda peer: to_peer(*passed_refs, peer).wait_send())
    for_peers(lambda peer: result_copy(peer).wait_send())
    for position in beside_columns:
        gain_copy(core, gain_send, gain_recv, position).wait_send()
        gain_copy(2, loss_send, loss_recv, position).wait_send()
        gain_arrival(position, core, share_send, share_recv).wait_send()


def local(adjoint_next, saved_state, gain_left, gain_right):
    share = adjoint_next.shape
    whole_field = pltpu.VMEM((8, 128, 256), jnp.float32)
    one_field = pltpu.VMEM((8, NV, 256), jnp.float32)
    dma = pltpu.SemaphoreType.DMA
    in_vmem = pl.BlockSpec(memory_space=pltpu.VMEM)
    anywhere = pl.BlockSpec(memory_space=pl.ANY)
    table = jnp.asarray(make_tables())
    return pl.pallas_call(
        kernel,
        out_shape=jax.ShapeDtypeStruct(share, jnp.float32),
        in_specs=[anywhere] * 6,
        out_specs=in_vmem,
        scratch_shapes=[
            pltpu.VMEM((TABLE_ROWS, 256), jnp.bfloat16),
            pltpu.VMEM((128, 128), jnp.float32),
            pltpu.VMEM(share, jnp.float32),
            pltpu.VMEM(share, jnp.float32),
            pltpu.VMEM(share, jnp.float32),
            pltpu.VMEM(share, jnp.float32),
            pltpu.VMEM((4, 16, 128), jnp.float32),
            pltpu.VMEM((4, 16, 128), jnp.float32),
            pltpu.VMEM((256, 128), jnp.float32),
            pltpu.VMEM((256, 128), jnp.float32),
            pltpu.VMEM((256, 128), jnp.float32),
            pltpu.VMEM((16, 16, 128), jnp.float32),
            pltpu.VMEM((2, NV, 1024), jnp.float32),
            pltpu.VMEM((3, 128, HALF), jnp.float32),
            pltpu.VMEM((2, 128, 512), jnp.float32),
            pltpu.VMEM((NV, HALF), jnp.float32),
            pltpu.VMEM((NV, 512), jnp.float32),
            one_field,
            one_field,
            one_field,
            one_field,
            whole_field,
            dma((6,)),
            dma((2,)),
            dma((16,)),
            dma((16,)),
            dma((16,)),
            dma((16,)),
            dma((16,)),
            dma((16,)),
            dma((4,)),
            dma((4,)),
            dma((4,)),
            dma((4,)),
            dma((4,)),
            dma((4,)),
        ],
        compiler_params=pltpu.CompilerParams(
            collective_id=0, has_side_effects=True, vmem_limit_bytes=60 * 1024 * 1024
        ),
        name="adjoint_step",
    )(adjoint_next, saved_state, gain_left, gain_right, table, jnp.asarray(make_twiddles()))


def solution(mesh):
    in_specs = (
        P("quad", None, "tile"),
        P("quad", None, "tile"),
        P("quad", None, None),
        P("quad", None, None),
    )
    out_specs = P("quad", None, "tile")
    return jax.shard_map(local, mesh=mesh, in_specs=in_specs, out_specs=out_specs, check_vma=False)
```

```python
import functools
import ml_dtypes
import numpy as np
import jax
import jax.numpy as jnp
from jax import lax
from jax.experimental import pallas as pl
from jax.experimental.pallas import tpu as pltpu
from jax.sharding import PartitionSpec as P

MESH = pl.DeviceIdType.MESH
NV = 32
BLOCK = 8
FARTHEST_FIRST = sorted(
    ((over, across) for over in range(4) for across in range(4) if over or across),
    key=lambda step: -(2 * min(step[0], 4 - step[0]) + min(step[1], 4 - step[1])),
)
HALF = 640
ROOT_HALF = float(np.sqrt(0.5))


def in_real_form(matrix):
    return np.block([[matrix.real, matrix.imag], [-matrix.imag, matrix.real]])


def two_halves(matrix):
    high = matrix.astype(ml_dtypes.bfloat16)
    low = (matrix - high.astype(np.float64)).astype(ml_dtypes.bfloat16)
    return high, low


def make_tables():
    steps = np.arange(NV)
    whole = np.exp(-2j * np.pi * (steps[:, None] * steps[None, :] % NV) / NV)
    four = np.arange(4)
    quarter = np.exp(-2j * np.pi * (four[:, None] * four[None, :] % 4) / 4)
    lanes = np.kron(quarter, whole)
    slots = np.kron(np.eye(4), whole)
    blocks = [
        in_real_form(lanes),
        in_real_form(slots),
        in_real_form(slots.conj() / NV),
        in_real_form(lanes.conj() / NV**2),
    ]
    rows = []
    for block in blocks:
        rows.extend(two_halves(block))
    back = whole.conj() / NV
    for left in (
        np.concatenate([whole.real, whole.imag], axis=0),
        np.concatenate([back.real, -back.imag], axis=1),
    ):
        high, low = two_halves(left)
        wide = np.concatenate([high, high, low], axis=1)
        rows.append(np.pad(wide, ((0, 0), (0, 256 - wide.shape[1]))))
    return np.concatenate(rows, axis=0)


def make_twiddles():
    angle = -2.0 * np.pi * (np.arange(8)[:, None] * (np.arange(128)[None, :] // 32)) / NV
    parts = np.stack([np.cos(angle), np.sin(angle)], axis=1).astype(np.float32)
    return np.broadcast_to(parts[:, :, None, :], (8, 2, 8, 128)).reshape(128, 128).copy()


ROWS_OF = {
    "lanes": (0, 256),
    "slots": (512, 768),
    "slots_back": (1024, 1280),
    "lanes_back": (1536, 1792),
}
LEFT_ROW = 2048
LEFT_BACK_ROW = 2112
TABLE_ROWS = 2144


def split(x):
    high = x.astype(jnp.bfloat16)
    low = (x - high.astype(jnp.float32)).astype(jnp.bfloat16)
    return high, low


def dot(a, b):
    return jnp.dot(a, b, preferred_element_type=jnp.float32)


def product(x, high, low):
    xh, xl = split(x)
    return dot(
        jnp.concatenate([xh, xl, xh], axis=1), jnp.concatenate([high, high, low], axis=0)
    )


def left_product(left, x):
    xh, xl = split(x)
    return dot(left, jnp.concatenate([xh, xl, xh], axis=0))


def turned(x):
    return jnp.concatenate([x[:, :128].T, x[:, 128:].T], axis=1)


def turn_by(value, factor):
    re, im = value
    fr, fi = factor
    return (re * fr - im * fi, re * fi + im * fr)


def plus(a, b):
    return (a[0] + b[0], a[1] + b[1])


def minus(a, b):
    return (a[0] - b[0], a[1] - b[1])


def four_points(x, sign):
    s0, d0 = plus(x[0], x[2]), minus(x[0], x[2])
    s1, d1 = plus(x[1], x[3]), minus(x[1], x[3])
    side = (-sign * d1[1], sign * d1[0]) if sign > 0 else (d1[1], -d1[0])
    return [plus(s0, s1), plus(d0, side), minus(s0, s1), minus(d0, side)]


def eight_points(x, sign):
    even = four_points(x[0::2], sign)
    odd = four_points(x[1::2], sign)
    o1, o2, o3 = odd[1], odd[2], odd[3]
    if sign < 0:
        o1 = ((o1[0] + o1[1]) * ROOT_HALF, (o1[1] - o1[0]) * ROOT_HALF)
        o2 = (o2[1], -o2[0])
        o3 = ((o3[1] - o3[0]) * ROOT_HALF, (o3[0] + o3[1]) * -ROOT_HALF)
    else:
        o1 = ((o1[0] - o1[1]) * ROOT_HALF, (o1[1] + o1[0]) * ROOT_HALF)
        o2 = (-o2[1], o2[0])
        o3 = ((o3[0] + o3[1]) * -ROOT_HALF, (o3[0] - o3[1]) * ROOT_HALF)
    odd = [odd[0], o1, o2, o3]
    return [plus(e, o) for e, o in zip(even, odd)] + [minus(e, o) for e, o in zip(even, odd)]


def forward_eight(x, factors):
    turned_x = [x[0]] + [turn_by(v, f) for v, f in zip(x[1:], factors)]
    return eight_points(turned_x, -1)


def backward_eight(x, factors):
    y = eight_points(x, 1)
    return [y[0]] + [turn_by(v, (fr, -fi)) for v, (fr, fi) in zip(y[1:], factors)]


def exchange_lanes(tiles):
    group = lax.broadcasted_iota(jnp.int32, (8, 128), 1) // 32
    upper = group >= 2
    odd = group % 2 == 1
    y = [None] * 4
    for h in range(2):
        y[h] = jnp.where(upper, pltpu.roll(tiles[h + 2], 64, 1), tiles[h])
        y[h + 2] = jnp.where(upper, tiles[h + 2], pltpu.roll(tiles[h], 64, 1))
    z = [None] * 4
    for h in (0, 2):
        z[h] = jnp.where(odd, pltpu.roll(y[h + 1], 32, 1), y[h])
        z[h + 1] = jnp.where(odd, y[h + 1], pltpu.roll(y[h], 96, 1))
    return z


def kernel(
    adjoint_hbm,
    state_hbm,
    gain_left,
    gain_right,
    table_hbm,
    twiddle_hbm,
    out,
    table,
    twiddles,
    adjoint,
    state,
    beside,
    passed_own,
    state_sent,
    passed_sent,
    state_all,
    passed_all,
    result,
    arrived,
    raw,
    gains,
    upper,
    loss_gain,
    loss_upper,
    spectrum,
    product_spectrum,
    total,
    loss,
    work,
    local_sem,
    halo_sem,
    state_send,
    state_recv,
    passed_send,
    passed_recv,
    result_send,
    result_recv,
    gain_send,
    gain_recv,
    share_send,
    share_recv,
    loss_send,
    loss_recv,
):
    tile = lax.axis_index("tile")
    quad = lax.axis_index("quad")
    tiles = lax.axis_size("tile")
    column = lax.rem(quad, 4)
    row = quad // 4
    core = lax.rem(tile, 2)
    sibling = tile + 1 - 2 * core
    ahead = quad >= 8
    up, down = lax.rem(tile + 1, tiles), lax.rem(tile + tiles - 1, tiles)
    source_tile = jnp.where(ahead, up, down)
    target_tile = jnp.where(ahead, down, up)

    barrier = pltpu.get_barrier_semaphore()

    for over, across in FARTHEST_FIRST:
        peer = lax.rem(row + over, 4) * 4 + lax.rem(column + across, 4)
        pl.semaphore_signal(barrier, inc=1, device_id={"quad": peer}, device_id_type=MESH)
    pl.semaphore_signal(barrier, inc=1, device_id={"tile": source_tile}, device_id_type=MESH)
    pl.semaphore_signal(barrier, inc=1, device_id={"tile": sibling}, device_id_type=MESH)

    fetch_twiddles = pltpu.make_async_copy(twiddle_hbm, twiddles, local_sem.at[5])
    fetch_table = pltpu.make_async_copy(table_hbm, table, local_sem.at[0])
    fetch_left = pltpu.make_async_copy(gain_left.at[0], raw.at[0], local_sem.at[1])
    fetch_right = pltpu.make_async_copy(gain_right.at[0], raw.at[1], local_sem.at[2])
    fetch_state = pltpu.make_async_copy(state_hbm, state, local_sem.at[3])
    fetch_adjoint = pltpu.make_async_copy(adjoint_hbm, adjoint, local_sem.at[4])
    fetch_state.start()
    fetch_adjoint.start()
    fetch_left.start()
    fetch_right.start()
    fetch_table.start()
    fetch_twiddles.start()

    fetch_left.wait()
    fetch_right.wait()
    lane = lax.broadcasted_iota(jnp.int32, (8, 128), 1)
    line = lax.broadcasted_iota(jnp.int32, (8, 128), 0)
    mirror_lane = lax.rem(4 - lane // 32, 4) * 32 + lax.rem(32 - lax.rem(lane, 32), 32)
    mirror_line = lax.rem(8 - line, 8)

    def mirrored(tile_of, h, r):
        def column(n):
            return jnp.where(lane < 32, tile_of((8 - h) % 8, n), tile_of((7 - h) % 8, n))

        rest = jnp.take_along_axis(column(3 - r), mirror_line, axis=0)
        both = jnp.where(line == 0, column((4 - r) % 4), rest)
        return jnp.take_along_axis(both, mirror_lane, axis=1)

    def raw_tile(kind):
        return lambda h, r: raw[kind, 8 * r : 8 * r + 8, 128 * h : 128 * h + 128]

    own_rows = column * 32
    for h in range(5):
        for r in range(4):
            at = pl.ds(own_rows + 8 * r, 8)
            here = slice(128 * h, 128 * h + 128)
            left, right = raw_tile(0)(h, r), raw_tile(1)(h, r)
            left_m, right_m = mirrored(raw_tile(0), h, r), mirrored(raw_tile(1), h, r)
            gains[0, at, here] = (left + left_m) * 0.5
            gains[1, at, here] = (right + right_m) * 0.5
            gains[2, at, here] = (left * right + left_m * right_m) * 0.5

    fetch_state.wait()
    for j in range(2):
        cells = exchange_lanes([state[j, 8 * h : 8 * h + 8, :] for h in range(4)])
        for cell in range(4):
            state_sent[cell, 8 * j : 8 * j + 8, :] = cells[cell]
    state_all[pl.ds(quad * 16, 16), :] = state_sent[column]

    pl.semaphore_wait(barrier, 17)

    halo = pltpu.make_async_remote_copy(
        src_ref=adjoint,
        dst_ref=beside,
        send_sem=halo_sem.at[0],
        recv_sem=halo_sem.at[1],
        device_id={"tile": target_tile},
        device_id_type=MESH,
    )
    fetch_adjoint.wait()
    halo.start()

    def to_peer(sent, whole, send, recv, peer):
        return pltpu.make_async_remote_copy(
            src_ref=sent.at[lax.rem(peer, 4)],
            dst_ref=whole.at[pl.ds(quad * 16, 16), :],
            send_sem=send.at[peer],
            recv_sem=recv.at[quad],
            device_id={"quad": peer},
            device_id_type=MESH,
        )

    def from_peer(sent, whole, send, recv, peer):
        return pltpu.make_async_remote_copy(
            src_ref=sent.at[0],
            dst_ref=whole.at[pl.ds(peer * 16, 16), :],
            send_sem=send.at[peer],
            recv_sem=recv.at[peer],
            device_id={"quad": peer},
            device_id_type=MESH,
        )

    def for_peers(action):
        for over, across in FARTHEST_FIRST:
            action(lax.rem(row + over, 4) * 4 + lax.rem(column + across, 4))

    state_refs = (state_sent, state_all, state_send, state_recv)
    passed_refs = (passed_sent, passed_all, passed_send, passed_recv)

    def gain_copy(kind, send, recv, position):
        return pltpu.make_async_remote_copy(
            src_ref=gains.at[kind, pl.ds(column * 32, 32), :],
            dst_ref=gains.at[kind, pl.ds(column * 32, 32), :],
            send_sem=send.at[position],
            recv_sem=recv.at[column],
            device_id={"quad": row * 4 + position},
            device_id_type=MESH,
        )

    def gain_arrival(position, kind, send, recv):
        return pltpu.make_async_remote_copy(
            src_ref=gains.at[kind, pl.ds(position * 32, 32), :],
            dst_ref=gains.at[kind, pl.ds(position * 32, 32), :],
            send_sem=send.at[position],
            recv_sem=recv.at[position],
            device_id={"tile": sibling},
            device_id_type=MESH,
        )

    beside_columns = [lax.rem(column + step, 4) for step in (2, 1, 3)]
    for position in beside_columns:
        gain_copy(core, gain_send, gain_recv, position).start()
    for_peers(lambda peer: to_peer(*state_refs, peer).start())

    halo.wait_recv()
    lower = lane < 64
    odd_cell = lane // 32 % 2 == 1
    from_own = jnp.logical_xor(lower, jnp.logical_not(ahead))
    for j in range(2):
        plane = (quad * 2 + j).astype(jnp.float32)
        speed_x = jnp.abs((plane - (NV - 1) / 2.0) / NV)
        for h in range(4):
            rows = slice(8 * h, 8 * h + 8)
            own = adjoint[j, rows, :]
            second = beside[j, rows, :]
            first = jnp.where(from_own, pltpu.roll(own, 64, 1), pltpu.roll(second, 64, 1))
            partner = jnp.where(odd_cell, pltpu.roll(own, 32, 1), pltpu.roll(own, 96, 1))
            b = (lax.broadcasted_iota(jnp.int32, (8, 128), 0) + 8 * h).astype(jnp.float32)
            speed_y = jnp.abs((b - (NV - 1) / 2.0) / NV)
            passed_own[j, rows, :] = (
                own
                - speed_x * (3.0 * own - 4.0 * first + second) * 0.5
                - 2.0 * speed_y * (own - partner)
            )
        cells = exchange_lanes([passed_own[j, 8 * h : 8 * h + 8, :] for h in range(4)])
        for cell in range(4):
            passed_sent[cell, 8 * j : 8 * j + 8, :] = cells[cell]
    passed_all[pl.ds(quad * 16, 16), :] = passed_sent[column]
    for_peers(lambda peer: to_peer(*passed_refs, peer).start())

    def tables(name):
        high, low = ROWS_OF[name]
        return table[high : high + 256, :], table[low : low + 256, :]

    def plane_of(ref, low_index):
        return ref[pl.ds(low_index, 32, stride=8), :]

    def tile_at(n):
        return slice(128 * n, 128 * n + 128)

    def factors():
        at = [slice(8 * n, 8 * n + 8) for n in range(16)]
        return [(twiddles[at[2 * n], :], twiddles[at[2 * n + 1], :]) for n in range(1, 8)]

    def load_eight(ref, rows):
        return [(ref[n, rows, :128], ref[n, rows, 128:]) for n in range(8)]

    def store_eight(ref, rows, values):
        for n, (re, im) in enumerate(values):
            ref[n, rows, :128] = re
            ref[n, rows, 128:] = im

    def eight_rows(start):
        return pl.ds(pl.multiple_of(start, 8), 8)

    def transform(planes, ref):
        left = table[LEFT_ROW : LEFT_ROW + 64, :96]
        mid = left_product(left, jnp.concatenate(planes, axis=1))
        rows = [
            jnp.concatenate([mid[:32, tile_at(n)], mid[32:, tile_at(n)]], axis=1) for n in range(8)
        ]
        ref[...] = product(jnp.concatenate(rows, axis=0), *tables("lanes")).reshape(8, NV, 256)

        def finish(r, carry):
            rows = eight_rows(8 * r)
            store_eight(ref, rows, forward_eight(load_eight(ref, rows), factors()))
            return carry

        lax.fori_loop(0, 4, finish, 0)

    fetch_table.wait()
    fetch_twiddles.wait()
    for_peers(lambda peer: from_peer(*state_refs, peer).wait_recv())
    transform([plane_of(state_all, n) for n in range(8)], spectrum)

    def unfold(kind):
        def body(pair, carry):
            def tile_of(h, r):
                return gains[kind, eight_rows(pair * 32 + 8 * r), tile_at(h)]

            for h in (7, 6, 5, 4):
                for r in range(4):
                    values = mirrored(tile_of, h, r)
                    if h == 4:
                        values = jnp.where(lane < 32, tile_of(4, r), values)
                    upper[kind, eight_rows(pair * 32 + 8 * r), tile_at(h - 4)] = values
            return carry

        lax.fori_loop(0, 4, body, 0)

    for position in beside_columns:
        gain_copy(2, loss_send, loss_recv, position).start()

    for position in beside_columns:
        gain_arrival(position, core, gain_send, gain_recv).wait_recv()
        gain_arrival(position, core, share_send, share_recv).start()
    unfold(core)

    def wait_passed():
        for_peers(lambda peer: from_peer(*passed_refs, peer).wait_recv())

    def transform_product():
        planes = [plane_of(state_all, n) * plane_of(passed_all, n) for n in range(8)]
        transform(planes, product_spectrum)

    wait_passed()
    transform_product()

    for position in beside_columns:
        gain_arrival(position, 1 - core, share_send, share_recv).wait_recv()
    unfold(1 - core)

    def gain_tile(kind, rows, n):
        return gains[kind, rows, tile_at(n)] if n < 4 else upper[kind, rows, tile_at(n - 4)]

    def filter_step(r, carry):
        rows = eight_rows(8 * r)
        both = []
        for n, (re, im) in enumerate(load_eight(spectrum, eight_rows(8 * lax.rem(r, 4)))):
            left, right = gain_tile(0, rows, n), gain_tile(1, rows, n)
            both.append((left * re - right * im, left * im + right * re))
        store_eight(work, rows, backward_eight(both, factors()))
        return carry

    lax.fori_loop(0, 16, filter_step, 0)

    def all_turned(values):
        parts = [turned(values[tile_at(n)]) for n in range(values.shape[0] // 128)]
        return jnp.concatenate(parts, axis=0)

    for i in range(0, 8, BLOCK):
        half = product(work[i : i + BLOCK].reshape(BLOCK * 128, 256), *tables("lanes_back"))
        fields = product(all_turned(half), *tables("slots_back"))
        work[i : i + BLOCK] = fields.reshape(BLOCK, 128, 256)

    for i in range(0, 8, BLOCK):
        crossed = []
        for n in range(i, i + BLOCK):
            weights = jnp.concatenate([plane_of(passed_all, n)] * 4, axis=0).T
            fields = work[n]
            crossed.append(
                jnp.concatenate([fields[:, 128:] * weights, fields[:, :128] * weights], axis=1)
            )
        half = product(jnp.concatenate(crossed, axis=0), *tables("slots"))
        fields = product(all_turned(half), *tables("lanes"))
        work[i : i + BLOCK] = fields.reshape(BLOCK, 128, 256)

    for position in beside_columns:
        gain_arrival(position, 2, loss_send, loss_recv).wait_recv()

    def loss_tile(h, r):
        return loss_gain[8 * r : 8 * r + 8, tile_at(h)]

    for r in range(4):
        for h in range(5):
            starts = [32 * pair + 8 * r for pair in range(4)]
            b = [gains[2, start : start + 8, tile_at(h)] for start in starts]
            loss_gain[8 * r : 8 * r + 8, tile_at(h)] = (b[0] + b[1]) + (b[2] + b[3])
    for h in (7, 6, 5, 4):
        for r in range(4):
            values = mirrored(loss_tile, h, r)
            if h == 4:
                values = jnp.where(lane < 32, loss_tile(4, r), values)
            loss_upper[8 * r : 8 * r + 8, tile_at(h - 4)] = values

    def total_step(r, carry):
        rows = eight_rows(8 * r)
        sums = []
        weights = [loss_gain[rows, tile_at(n)] for n in range(4)]
        weights += [loss_upper[rows, tile_at(n)] for n in range(4)]
        for n, (re, im) in enumerate(load_eight(product_spectrum, rows)):
            sums.append((-weights[n] * re, -weights[n] * im))
        for pair in range(4):
            at = eight_rows(32 * pair + 8 * r)
            for n, (re, im) in enumerate(forward_eight(load_eight(work, at), factors())):
                left, right = gain_tile(0, at, n), gain_tile(1, at, n)
                sums[n] = (
                    sums[n][0] + (left * re + right * im),
                    sums[n][1] + (left * im - right * re),
                )
        store_eight(total, rows, backward_eight(sums, factors()))
        lost = [
            (weights[n] * re, weights[n] * im)
            for n, (re, im) in enumerate(load_eight(spectrum, rows))
        ]
        store_eight(loss, rows, backward_eight(lost, factors()))
        return carry

    lax.fori_loop(0, 4, total_step, 0)

    both = jnp.concatenate([total[...].reshape(256, 256), loss[...].reshape(256, 256)], axis=0)
    both = product(both, *tables("lanes_back"))

    def last_axis(values):
        parts = [values[32 * n : 32 * n + 32] for n in range(8)]
        re = jnp.concatenate([part[:, :128] for part in parts], axis=1)
        im = jnp.concatenate([part[:, 128:] for part in parts], axis=1)
        left = table[LEFT_BACK_ROW : LEFT_BACK_ROW + 32, :192]
        return left_product(left, jnp.concatenate([re, im], axis=0))

    gained, lost = last_axis(both[:256]), last_axis(both[256:])
    for n in range(8):
        value = gained[:, tile_at(n)] - plane_of(passed_all, n) * lost[:, tile_at(n)]
        result[pl.ds(n, 32, stride=8), :] = value

    def result_copy(peer):
        return pltpu.make_async_remote_copy(
            src_ref=result.at[pl.ds(peer * 16, 16), :],
            dst_ref=arrived.at[quad],
            send_sem=result_send.at[peer],
            recv_sem=result_recv.at[quad],
            device_id={"quad": peer},
            device_id_type=MESH,
        )

    def result_arrival(peer):
        return pltpu.make_async_remote_copy(
            src_ref=result.at[pl.ds(peer * 16, 16), :],
            dst_ref=arrived.at[peer],
            send_sem=result_send.at[peer],
            recv_sem=result_recv.at[peer],
            device_id={"quad": peer},
            device_id_type=MESH,
        )

    for_peers(lambda peer: result_copy(peer).start())
    arrived[quad] = result[pl.ds(quad * 16, 16), :]
    for_peers(lambda peer: result_arrival(peer).wait_recv())

    for j in range(2):
        rows = slice(8 * j, 8 * j + 8)
        cells = [
            arrived[cell, rows, :]
            + arrived[4 + cell, rows, :]
            + arrived[8 + cell, rows, :]
            + arrived[12 + cell, rows, :]
            for cell in range(4)
        ]
        parts = exchange_lanes(cells)
        for h in range(4):
            part = slice(8 * h, 8 * h + 8)
            out[j, part, :] = passed_own[j, part, :] + parts[h] * (1.0 / 16.0)

    halo.wait_send()
    for_peers(lambda peer: to_peer(*state_refs, peer).wait_send())
    for_peers(lambda peer: to_peer(*passed_refs, peer).wait_send())
    for_peers(lambda peer: result_copy(peer).wait_send())
    for position in beside_columns:
        gain_copy(core, gain_send, gain_recv, position).wait_send()
        gain_copy(2, loss_send, loss_recv, position).wait_send()
        gain_arrival(position, core, share_send, share_recv).wait_send()


def local(adjoint_next, saved_state, gain_left, gain_right):
    share = adjoint_next.shape
    whole_field = pltpu.VMEM((8, 128, 256), jnp.float32)
    one_field = pltpu.VMEM((8, NV, 256), jnp.float32)
    dma = pltpu.SemaphoreType.DMA
    in_vmem = pl.BlockSpec(memory_space=pltpu.VMEM)
    anywhere = pl.BlockSpec(memory_space=pl.ANY)
    table = jnp.asarray(make_tables())
    return pl.pallas_call(
        kernel,
        out_shape=jax.ShapeDtypeStruct(share, jnp.float32),
        in_specs=[anywhere] * 6,
        out_specs=in_vmem,
        scratch_shapes=[
            pltpu.VMEM((TABLE_ROWS, 256), jnp.bfloat16),
            pltpu.VMEM((128, 128), jnp.float32),
            pltpu.VMEM(share, jnp.float32),
            pltpu.VMEM(share, jnp.float32),
            pltpu.VMEM(share, jnp.float32),
            pltpu.VMEM(share, jnp.float32),
            pltpu.VMEM((4, 16, 128), jnp.float32),
            pltpu.VMEM((4, 16, 128), jnp.float32),
            pltpu.VMEM((256, 128), jnp.float32),
            pltpu.VMEM((256, 128), jnp.float32),
            pltpu.VMEM((256, 128), jnp.float32),
            pltpu.VMEM((16, 16, 128), jnp.float32),
            pltpu.VMEM((2, NV, 1024), jnp.float32),
            pltpu.VMEM((3, 128, HALF), jnp.float32),
            pltpu.VMEM((2, 128, 512), jnp.float32),
            pltpu.VMEM((NV, HALF), jnp.float32),
            pltpu.VMEM((NV, 512), jnp.float32),
            one_field,
            one_field,
            one_field,
            one_field,
            whole_field,
            dma((6,)),
            dma((2,)),
            dma((16,)),
            dma((16,)),
            dma((16,)),
            dma((16,)),
            dma((16,)),
            dma((16,)),
            dma((4,)),
            dma((4,)),
            dma((4,)),
            dma((4,)),
            dma((4,)),
            dma((4,)),
        ],
        compiler_params=pltpu.CompilerParams(
            collective_id=0, has_side_effects=True, vmem_limit_bytes=60 * 1024 * 1024
        ),
        name="adjoint_step",
    )(adjoint_next, saved_state, gain_left, gain_right, table, jnp.asarray(make_twiddles()))


def solution(mesh):
    in_specs = (
        P("quad", None, "tile"),
        P("quad", None, "tile"),
        P("quad", None, None),
        P("quad", None, None),
    )
    out_specs = P("quad", None, "tile")
    return jax.shard_map(local, mesh=mesh, in_specs=in_specs, out_specs=out_specs, check_vma=False)
```

```python
import functools
import ml_dtypes
import numpy as np
import jax
import jax.numpy as jnp
from jax import lax
from jax.experimental import pallas as pl
from jax.experimental.pallas import tpu as pltpu
from jax.sharding import PartitionSpec as P

MESH = pl.DeviceIdType.MESH
NV = 32
BLOCK = 8
FARTHEST_FIRST = sorted(
    ((over, across) for over in range(4) for across in range(4)),
    key=lambda step: -(2 * min(step[0], 4 - step[0]) + min(step[1], 4 - step[1])),
)
HALF = 640
ROOT_HALF = float(np.sqrt(0.5))


def in_real_form(matrix):
    return np.block([[matrix.real, matrix.imag], [-matrix.imag, matrix.real]])


def two_halves(matrix):
    high = matrix.astype(ml_dtypes.bfloat16)
    low = (matrix - high.astype(np.float64)).astype(ml_dtypes.bfloat16)
    return high, low


def make_tables():
    steps = np.arange(NV)
    whole = np.exp(-2j * np.pi * (steps[:, None] * steps[None, :] % NV) / NV)
    four = np.arange(4)
    quarter = np.exp(-2j * np.pi * (four[:, None] * four[None, :] % 4) / 4)
    lanes = np.kron(quarter, whole)
    slots = np.kron(np.eye(4), whole)
    blocks = [
        in_real_form(lanes),
        in_real_form(slots),
        in_real_form(slots.conj() / NV),
        in_real_form(lanes.conj() / NV**2),
    ]
    rows = []
    for block in blocks:
        rows.extend(two_halves(block))
    back = whole.conj() / NV
    for left in (
        np.concatenate([whole.real, whole.imag], axis=0),
        np.concatenate([back.real, -back.imag], axis=1),
    ):
        high, low = two_halves(left)
        wide = np.concatenate([high, high, low], axis=1)
        rows.append(np.pad(wide, ((0, 0), (0, 256 - wide.shape[1]))))
    return np.concatenate(rows, axis=0)


def make_twiddles():
    angle = -2.0 * np.pi * (np.arange(8)[:, None] * (np.arange(128)[None, :] // 32)) / NV
    parts = np.stack([np.cos(angle), np.sin(angle)], axis=1).astype(np.float32)
    return np.broadcast_to(parts[:, :, None, :], (8, 2, 8, 128)).reshape(128, 128).copy()


ROWS_OF = {
    "lanes": (0, 256),
    "slots": (512, 768),
    "slots_back": (1024, 1280),
    "lanes_back": (1536, 1792),
}
LEFT_ROW = 2048
LEFT_BACK_ROW = 2112
TABLE_ROWS = 2144


def split(x):
    high = x.astype(jnp.bfloat16)
    low = (x - high.astype(jnp.float32)).astype(jnp.bfloat16)
    return high, low


def dot(a, b):
    return jnp.dot(a, b, preferred_element_type=jnp.float32)


def product(x, high, low):
    xh, xl = split(x)
    return dot(
        jnp.concatenate([xh, xl, xh], axis=1), jnp.concatenate([high, high, low], axis=0)
    )


def left_product(left, x):
    xh, xl = split(x)
    return dot(left, jnp.concatenate([xh, xl, xh], axis=0))


def turned(x):
    return jnp.concatenate([x[:, :128].T, x[:, 128:].T], axis=1)


def turn_by(value, factor):
    re, im = value
    fr, fi = factor
    return (re * fr - im * fi, re * fi + im * fr)


def plus(a, b):
    return (a[0] + b[0], a[1] + b[1])


def minus(a, b):
    return (a[0] - b[0], a[1] - b[1])


def four_points(x, sign):
    s0, d0 = plus(x[0], x[2]), minus(x[0], x[2])
    s1, d1 = plus(x[1], x[3]), minus(x[1], x[3])
    side = (-sign * d1[1], sign * d1[0]) if sign > 0 else (d1[1], -d1[0])
    return [plus(s0, s1), plus(d0, side), minus(s0, s1), minus(d0, side)]


def eight_points(x, sign):
    even = four_points(x[0::2], sign)
    odd = four_points(x[1::2], sign)
    o1, o2, o3 = odd[1], odd[2], odd[3]
    if sign < 0:
        o1 = ((o1[0] + o1[1]) * ROOT_HALF, (o1[1] - o1[0]) * ROOT_HALF)
        o2 = (o2[1], -o2[0])
        o3 = ((o3[1] - o3[0]) * ROOT_HALF, (o3[0] + o3[1]) * -ROOT_HALF)
    else:
        o1 = ((o1[0] - o1[1]) * ROOT_HALF, (o1[1] + o1[0]) * ROOT_HALF)
        o2 = (-o2[1], o2[0])
        o3 = ((o3[0] + o3[1]) * -ROOT_HALF, (o3[0] - o3[1]) * ROOT_HALF)
    odd = [odd[0], o1, o2, o3]
    return [plus(e, o) for e, o in zip(even, odd)] + [minus(e, o) for e, o in zip(even, odd)]


def forward_eight(x, factors):
    turned_x = [x[0]] + [turn_by(v, f) for v, f in zip(x[1:], factors)]
    return eight_points(turned_x, -1)


def backward_eight(x, factors):
    y = eight_points(x, 1)
    return [y[0]] + [turn_by(v, (fr, -fi)) for v, (fr, fi) in zip(y[1:], factors)]


def exchange_lanes(tiles):
    group = lax.broadcasted_iota(jnp.int32, (8, 128), 1) // 32
    upper = group >= 2
    odd = group % 2 == 1
    y = [None] * 4
    for h in range(2):
        y[h] = jnp.where(upper, pltpu.roll(tiles[h + 2], 64, 1), tiles[h])
        y[h + 2] = jnp.where(upper, tiles[h + 2], pltpu.roll(tiles[h], 64, 1))
    z = [None] * 4
    for h in (0, 2):
        z[h] = jnp.where(odd, pltpu.roll(y[h + 1], 32, 1), y[h])
        z[h + 1] = jnp.where(odd, y[h + 1], pltpu.roll(y[h], 96, 1))
    return z


def kernel(
    adjoint_hbm,
    state_hbm,
    gain_left,
    gain_right,
    table_hbm,
    twiddle_hbm,
    out,
    table,
    twiddles,
    adjoint,
    state,
    beside,
    passed_own,
    state_sent,
    passed_sent,
    state_all,
    passed_all,
    result,
    arrived,
    raw,
    gains,
    upper,
    loss_gain,
    loss_upper,
    spectrum,
    product_spectrum,
    total,
    loss,
    work,
    local_sem,
    halo_sem,
    state_send,
    state_recv,
    passed_send,
    passed_recv,
    result_send,
    result_recv,
    gain_send,
    gain_recv,
    share_send,
    share_recv,
    loss_send,
    loss_recv,
    near_here,
    far_here,
):
    tile = lax.axis_index("tile")
    quad = lax.axis_index("quad")
    tiles = lax.axis_size("tile")
    column = lax.rem(quad, 4)
    row = quad // 4
    core = lax.rem(tile, 2)
    sibling = tile + 1 - 2 * core
    partner_tile = lax.rem(tile + tiles // 2, tiles)
    ahead = quad >= 8
    up, down = lax.rem(tile + 1, tiles), lax.rem(tile + tiles - 1, tiles)
    source_tile = jnp.where(ahead, up, down)
    target_tile = jnp.where(ahead, down, up)

    barrier = pltpu.get_barrier_semaphore()
    even_tile = tile - core
    far_listener = partner_tile - core + 1
    for over, across in FARTHEST_FIRST:
        peer = lax.rem(row + over, 4) * 4 + lax.rem(column + across, 4)
        pl.semaphore_signal(
            barrier, inc=1, device_id={"tile": far_listener, "quad": peer}, device_id_type=MESH
        )
    for step in (2, 1, 3):
        peer = row * 4 + lax.rem(column + step, 4)
        pl.semaphore_signal(
            barrier, inc=1, device_id={"tile": even_tile, "quad": peer}, device_id_type=MESH
        )
    near_source = source_tile - lax.rem(source_tile, 2)

    @pl.when(near_source != tile)
    def _():
        pl.semaphore_signal(barrier, inc=1, device_id={"tile": near_source}, device_id_type=MESH)

    @pl.when(core == 1)
    def _():
        pl.semaphore_signal(barrier, inc=1, device_id={"tile": sibling}, device_id_type=MESH)

    fetch_twiddles = pltpu.make_async_copy(twiddle_hbm, twiddles, local_sem.at[5])
    fetch_table = pltpu.make_async_copy(table_hbm, table, local_sem.at[0])
    fetch_left = pltpu.make_async_copy(gain_left.at[0], raw.at[0], local_sem.at[1])
    fetch_right = pltpu.make_async_copy(gain_right.at[0], raw.at[1], local_sem.at[2])
    fetch_state = pltpu.make_async_copy(state_hbm, state, local_sem.at[3])
    fetch_adjoint = pltpu.make_async_copy(adjoint_hbm, adjoint, local_sem.at[4])
    fetch_state.start()
    fetch_adjoint.start()
    fetch_left.start()
    fetch_right.start()
    fetch_table.start()
    fetch_twiddles.start()

    fetch_left.wait()
    fetch_right.wait()
    lane = lax.broadcasted_iota(jnp.int32, (8, 128), 1)
    line = lax.broadcasted_iota(jnp.int32, (8, 128), 0)
    mirror_lane = lax.rem(4 - lane // 32, 4) * 32 + lax.rem(32 - lax.rem(lane, 32), 32)
    mirror_line = lax.rem(8 - line, 8)

    def mirrored(tile_of, h, r):
        def column(n):
            return jnp.where(lane < 32, tile_of((8 - h) % 8, n), tile_of((7 - h) % 8, n))

        rest = jnp.take_along_axis(column(3 - r), mirror_line, axis=0)
        both = jnp.where(line == 0, column((4 - r) % 4), rest)
        return jnp.take_along_axis(both, mirror_lane, axis=1)

    def raw_tile(kind):
        return lambda h, r: raw[kind, 8 * r : 8 * r + 8, 128 * h : 128 * h + 128]

    own_rows = column * 32
    for h in range(5):
        for r in range(4):
            at = pl.ds(own_rows + 8 * r, 8)
            here = slice(128 * h, 128 * h + 128)
            left, right = raw_tile(0)(h, r), raw_tile(1)(h, r)
            left_m, right_m = mirrored(raw_tile(0), h, r), mirrored(raw_tile(1), h, r)
            gains[0, at, here] = (left + left_m) * 0.5
            gains[1, at, here] = (right + right_m) * 0.5
            gains[2, at, here] = (left * right + left_m * right_m) * 0.5

    fetch_state.wait()
    for j in range(2):
        cells = exchange_lanes([state[j, 8 * h : 8 * h + 8, :] for h in range(4)])
        for cell in range(4):
            state_sent[cell, 8 * j : 8 * j + 8, :] = cells[cell]

    @pl.when(core == 0)
    def _():
        pl.semaphore_wait(barrier, jnp.where(ahead, 8, 9))
        pl.semaphore_signal(near_here, inc=1, device_id={"tile": sibling}, device_id_type=MESH)

    @pl.when(core == 1)
    def _():
        pl.semaphore_wait(near_here, 1)

    halo = pltpu.make_async_remote_copy(
        src_ref=adjoint,
        dst_ref=beside,
        send_sem=halo_sem.at[0],
        recv_sem=halo_sem.at[1],
        device_id={"tile": target_tile},
        device_id_type=MESH,
    )
    fetch_adjoint.wait()
    halo.start()

    def to_peer(sent, whole, send, recv, peer):
        return pltpu.make_async_remote_copy(
            src_ref=sent.at[lax.rem(peer, 4)],
            dst_ref=whole.at[pl.ds(quad * 16, 16), :],
            send_sem=send.at[peer],
            recv_sem=recv.at[quad],
            device_id={"tile": partner_tile, "quad": peer},
            device_id_type=MESH,
        )

    def from_peer(sent, whole, send, recv, peer):
        return pltpu.make_async_remote_copy(
            src_ref=sent.at[0],
            dst_ref=whole.at[pl.ds(peer * 16, 16), :],
            send_sem=send.at[peer],
            recv_sem=recv.at[peer],
            device_id={"tile": partner_tile, "quad": peer},
            device_id_type=MESH,
        )

    def for_peers(action):
        for over, across in FARTHEST_FIRST:
            action(lax.rem(row + over, 4) * 4 + lax.rem(column + across, 4))

    state_refs = (state_sent, state_all, state_send, state_recv)
    passed_refs = (passed_sent, passed_all, passed_send, passed_recv)

    def gain_copy(kind, send, recv, position):
        return pltpu.make_async_remote_copy(
            src_ref=gains.at[kind, pl.ds(column * 32, 32), :],
            dst_ref=gains.at[kind, pl.ds(column * 32, 32), :],
            send_sem=send.at[position],
            recv_sem=recv.at[column],
            device_id={"quad": row * 4 + position},
            device_id_type=MESH,
        )

    def gain_arrival(position, kind, send, recv):
        return pltpu.make_async_remote_copy(
            src_ref=gains.at[kind, pl.ds(position * 32, 32), :],
            dst_ref=gains.at[kind, pl.ds(position * 32, 32), :],
            send_sem=send.at[position],
            recv_sem=recv.at[position],
            device_id={"tile": sibling},
            device_id_type=MESH,
        )

    beside_columns = [lax.rem(column + step, 4) for step in (2, 1, 3)]
    for position in beside_columns:
        gain_copy(core, gain_send, gain_recv, position).start()

    @pl.when(core == 1)
    def _():
        pl.semaphore_wait(barrier, 32)
        pl.semaphore_signal(far_here, inc=1, device_id={"tile": sibling}, device_id_type=MESH)

    @pl.when(core == 0)
    def _():
        pl.semaphore_wait(far_here, 1)

    for_peers(lambda peer: to_peer(*state_refs, peer).start())

    halo.wait_recv()
    lower = lane < 64
    odd_cell = lane // 32 % 2 == 1
    from_own = jnp.logical_xor(lower, jnp.logical_not(ahead))
    for j in range(2):
        plane = (quad * 2 + j).astype(jnp.float32)
        speed_x = jnp.abs((plane - (NV - 1) / 2.0) / NV)
        for h in range(4):
            rows = slice(8 * h, 8 * h + 8)
            own = adjoint[j, rows, :]
            second = beside[j, rows, :]
            first = jnp.where(from_own, pltpu.roll(own, 64, 1), pltpu.roll(second, 64, 1))
            partner = jnp.where(odd_cell, pltpu.roll(own, 32, 1), pltpu.roll(own, 96, 1))
            b = (lax.broadcasted_iota(jnp.int32, (8, 128), 0) + 8 * h).astype(jnp.float32)
            speed_y = jnp.abs((b - (NV - 1) / 2.0) / NV)
            passed_own[j, rows, :] = (
                own
                - speed_x * (3.0 * own - 4.0 * first + second) * 0.5
                - 2.0 * speed_y * (own - partner)
            )
        cells = exchange_lanes([passed_own[j, 8 * h : 8 * h + 8, :] for h in range(4)])
        for cell in range(4):
            passed_sent[cell, 8 * j : 8 * j + 8, :] = cells[cell]
    for_peers(lambda peer: to_peer(*passed_refs, peer).start())

    def tables(name):
        high, low = ROWS_OF[name]
        return table[high : high + 256, :], table[low : low + 256, :]

    def plane_of(ref, low_index):
        return ref[pl.ds(low_index, 32, stride=8), :]

    def tile_at(n):
        return slice(128 * n, 128 * n + 128)

    def factors():
        at = [slice(8 * n, 8 * n + 8) for n in range(16)]
        return [(twiddles[at[2 * n], :], twiddles[at[2 * n + 1], :]) for n in range(1, 8)]

    def load_eight(ref, rows):
        return [(ref[n, rows, :128], ref[n, rows, 128:]) for n in range(8)]

    def store_eight(ref, rows, values):
        for n, (re, im) in enumerate(values):
            ref[n, rows, :128] = re
            ref[n, rows, 128:] = im

    def eight_rows(start):
        return pl.ds(pl.multiple_of(start, 8), 8)

    def transform(planes, ref):
        left = table[LEFT_ROW : LEFT_ROW + 64, :96]
        mid = left_product(left, jnp.concatenate(planes, axis=1))
        rows = [
            jnp.concatenate([mid[:32, tile_at(n)], mid[32:, tile_at(n)]], axis=1) for n in range(8)
        ]
        ref[...] = product(jnp.concatenate(rows, axis=0), *tables("lanes")).reshape(8, NV, 256)

        def finish(r, carry):
            rows = eight_rows(8 * r)
            store_eight(ref, rows, forward_eight(load_eight(ref, rows), factors()))
            return carry

        lax.fori_loop(0, 4, finish, 0)

    fetch_table.wait()
    fetch_twiddles.wait()
    for_peers(lambda peer: from_peer(*state_refs, peer).wait_recv())
    transform([plane_of(state_all, n) for n in range(8)], spectrum)

    def unfold(kind):
        def body(pair, carry):
            def tile_of(h, r):
                return gains[kind, eight_rows(pair * 32 + 8 * r), tile_at(h)]

            for h in (7, 6, 5, 4):
                for r in range(4):
                    values = mirrored(tile_of, h, r)
                    if h == 4:
                        values = jnp.where(lane < 32, tile_of(4, r), values)
                    upper[kind, eight_rows(pair * 32 + 8 * r), tile_at(h - 4)] = values
            return carry

        lax.fori_loop(0, 4, body, 0)

    for position in beside_columns:
        gain_copy(2, loss_send, loss_recv, position).start()

    for position in beside_columns:
        gain_arrival(position, core, gain_send, gain_recv).wait_recv()
        gain_arrival(position, core, share_send, share_recv).start()
    unfold(core)

    def wait_passed():
        for_peers(lambda peer: from_peer(*passed_refs, peer).wait_recv())

    def transform_product():
        planes = [plane_of(state_all, n) * plane_of(passed_all, n) for n in range(8)]
        transform(planes, product_spectrum)

    wait_passed()
    transform_product()

    for position in beside_columns:
        gain_arrival(position, 1 - core, share_send, share_recv).wait_recv()
    unfold(1 - core)

    def gain_tile(kind, rows, n):
        return gains[kind, rows, tile_at(n)] if n < 4 else upper[kind, rows, tile_at(n - 4)]

    def filter_step(r, carry):
        rows = eight_rows(8 * r)
        both = []
        for n, (re, im) in enumerate(load_eight(spectrum, eight_rows(8 * lax.rem(r, 4)))):
            left, right = gain_tile(0, rows, n), gain_tile(1, rows, n)
            both.append((left * re - right * im, left * im + right * re))
        store_eight(work, rows, backward_eight(both, factors()))
        return carry

    lax.fori_loop(0, 16, filter_step, 0)

    def all_turned(values):
        parts = [turned(values[tile_at(n)]) for n in range(values.shape[0] // 128)]
        return jnp.concatenate(parts, axis=0)

    for i in range(0, 8, BLOCK):
        half = product(work[i : i + BLOCK].reshape(BLOCK * 128, 256), *tables("lanes_back"))
        fields = product(all_turned(half), *tables("slots_back"))
        work[i : i + BLOCK] = fields.reshape(BLOCK, 128, 256)

    for i in range(0, 8, BLOCK):
        crossed = []
        for n in range(i, i + BLOCK):
            weights = jnp.concatenate([plane_of(passed_all, n)] * 4, axis=0).T
            fields = work[n]
            crossed.append(
                jnp.concatenate([fields[:, 128:] * weights, fields[:, :128] * weights], axis=1)
            )
        half = product(jnp.concatenate(crossed, axis=0), *tables("slots"))
        fields = product(all_turned(half), *tables("lanes"))
        work[i : i + BLOCK] = fields.reshape(BLOCK, 128, 256)

    for position in beside_columns:
        gain_arrival(position, 2, loss_send, loss_recv).wait_recv()

    def loss_tile(h, r):
        return loss_gain[8 * r : 8 * r + 8, tile_at(h)]

    for r in range(4):
        for h in range(5):
            starts = [32 * pair + 8 * r for pair in range(4)]
            b = [gains[2, start : start + 8, tile_at(h)] for start in starts]
            loss_gain[8 * r : 8 * r + 8, tile_at(h)] = (b[0] + b[1]) + (b[2] + b[3])
    for h in (7, 6, 5, 4):
        for r in range(4):
            values = mirrored(loss_tile, h, r)
            if h == 4:
                values = jnp.where(lane < 32, loss_tile(4, r), values)
            loss_upper[8 * r : 8 * r + 8, tile_at(h - 4)] = values

    def total_step(r, carry):
        rows = eight_rows(8 * r)
        sums = []
        weights = [loss_gain[rows, tile_at(n)] for n in range(4)]
        weights += [loss_upper[rows, tile_at(n)] for n in range(4)]
        for n, (re, im) in enumerate(load_eight(product_spectrum, rows)):
            sums.append((-weights[n] * re, -weights[n] * im))
        for pair in range(4):
            at = eight_rows(32 * pair + 8 * r)
            for n, (re, im) in enumerate(forward_eight(load_eight(work, at), factors())):
                left, right = gain_tile(0, at, n), gain_tile(1, at, n)
                sums[n] = (
                    sums[n][0] + (left * re + right * im),
                    sums[n][1] + (left * im - right * re),
                )
        store_eight(total, rows, backward_eight(sums, factors()))
        lost = [
            (weights[n] * re, weights[n] * im)
            for n, (re, im) in enumerate(load_eight(spectrum, rows))
        ]
        store_eight(loss, rows, backward_eight(lost, factors()))
        return carry

    lax.fori_loop(0, 4, total_step, 0)

    both = jnp.concatenate([total[...].reshape(256, 256), loss[...].reshape(256, 256)], axis=0)
    both = product(both, *tables("lanes_back"))

    def last_axis(values):
        parts = [values[32 * n : 32 * n + 32] for n in range(8)]
        re = jnp.concatenate([part[:, :128] for part in parts], axis=1)
        im = jnp.concatenate([part[:, 128:] for part in parts], axis=1)
        left = table[LEFT_BACK_ROW : LEFT_BACK_ROW + 32, :192]
        return left_product(left, jnp.concatenate([re, im], axis=0))

    gained, lost = last_axis(both[:256]), last_axis(both[256:])
    for n in range(8):
        value = gained[:, tile_at(n)] - plane_of(passed_all, n) * lost[:, tile_at(n)]
        result[pl.ds(n, 32, stride=8), :] = value

    def result_copy(peer):
        return pltpu.make_async_remote_copy(
            src_ref=result.at[pl.ds(peer * 16, 16), :],
            dst_ref=arrived.at[quad],
            send_sem=result_send.at[peer],
            recv_sem=result_recv.at[quad],
            device_id={"tile": partner_tile, "quad": peer},
            device_id_type=MESH,
        )

    def result_arrival(peer):
        return pltpu.make_async_remote_copy(
            src_ref=result.at[pl.ds(peer * 16, 16), :],
            dst_ref=arrived.at[peer],
            send_sem=result_send.at[peer],
            recv_sem=result_recv.at[peer],
            device_id={"tile": partner_tile, "quad": peer},
            device_id_type=MESH,
        )

    for_peers(lambda peer: result_copy(peer).start())
    for_peers(lambda peer: result_arrival(peer).wait_recv())

    for j in range(2):
        rows = slice(8 * j, 8 * j + 8)
        cells = [
            arrived[cell, rows, :]
            + arrived[4 + cell, rows, :]
            + arrived[8 + cell, rows, :]
            + arrived[12 + cell, rows, :]
            for cell in range(4)
        ]
        parts = exchange_lanes(cells)
        for h in range(4):
            part = slice(8 * h, 8 * h + 8)
            out[j, part, :] = passed_own[j, part, :] + parts[h] * (1.0 / 16.0)

    halo.wait_send()
    for_peers(lambda peer: to_peer(*state_refs, peer).wait_send())
    for_peers(lambda peer: to_peer(*passed_refs, peer).wait_send())
    for_peers(lambda peer: result_copy(peer).wait_send())
    for position in beside_columns:
        gain_copy(core, gain_send, gain_recv, position).wait_send()
        gain_copy(2, loss_send, loss_recv, position).wait_send()
        gain_arrival(position, core, share_send, share_recv).wait_send()


def local(adjoint_next, saved_state, gain_left, gain_right):
    share = adjoint_next.shape
    whole_field = pltpu.VMEM((8, 128, 256), jnp.float32)
    one_field = pltpu.VMEM((8, NV, 256), jnp.float32)
    dma = pltpu.SemaphoreType.DMA
    in_vmem = pl.BlockSpec(memory_space=pltpu.VMEM)
    anywhere = pl.BlockSpec(memory_space=pl.ANY)
    table = jnp.asarray(make_tables())
    return pl.pallas_call(
        kernel,
        out_shape=jax.ShapeDtypeStruct(share, jnp.float32),
        in_specs=[anywhere] * 6,
        out_specs=in_vmem,
        scratch_shapes=[
            pltpu.VMEM((TABLE_ROWS, 256), jnp.bfloat16),
            pltpu.VMEM((128, 128), jnp.float32),
            pltpu.VMEM(share, jnp.float32),
            pltpu.VMEM(share, jnp.float32),
            pltpu.VMEM(share, jnp.float32),
            pltpu.VMEM(share, jnp.float32),
            pltpu.VMEM((4, 16, 128), jnp.float32),
            pltpu.VMEM((4, 16, 128), jnp.float32),
            pltpu.VMEM((256, 128), jnp.float32),
            pltpu.VMEM((256, 128), jnp.float32),
            pltpu.VMEM((256, 128), jnp.float32),
            pltpu.VMEM((16, 16, 128), jnp.float32),
            pltpu.VMEM((2, NV, 1024), jnp.float32),
            pltpu.VMEM((3, 128, HALF), jnp.float32),
            pltpu.VMEM((2, 128, 512), jnp.float32),
            pltpu.VMEM((NV, HALF), jnp.float32),
            pltpu.VMEM((NV, 512), jnp.float32),
            one_field,
            one_field,
            one_field,
            one_field,
            whole_field,
            dma((6,)),
            dma((2,)),
            dma((16,)),
            dma((16,)),
            dma((16,)),
            dma((16,)),
            dma((16,)),
            dma((16,)),
            dma((4,)),
            dma((4,)),
            dma((4,)),
            dma((4,)),
            dma((4,)),
            dma((4,)),
            pltpu.SemaphoreType.REGULAR,
            pltpu.SemaphoreType.REGULAR,
        ],
        compiler_params=pltpu.CompilerParams(
            collective_id=0, has_side_effects=True, vmem_limit_bytes=60 * 1024 * 1024
        ),
        name="adjoint_step",
    )(adjoint_next, saved_state, gain_left, gain_right, table, jnp.asarray(make_twiddles()))


def solution(mesh):
    in_specs = (
        P("quad", None, "tile"),
        P("quad", None, "tile"),
        P("quad", None, None),
        P("quad", None, None),
    )
    out_specs = P("quad", None, "tile")
    return jax.shard_map(local, mesh=mesh, in_specs=in_specs, out_specs=out_specs, check_vma=False)
```

```python
import functools
import ml_dtypes
import numpy as np
import jax
import jax.numpy as jnp
from jax import lax
from jax.experimental import pallas as pl
from jax.experimental.pallas import tpu as pltpu
from jax.sharding import PartitionSpec as P

MESH = pl.DeviceIdType.MESH
NV = 32
BLOCK = 8
FARTHEST_FIRST = sorted(
    ((over, across) for over in range(4) for across in range(4)),
    key=lambda step: -(2 * min(step[0], 4 - step[0]) + min(step[1], 4 - step[1])),
)
HALF = 640
ROOT_HALF = float(np.sqrt(0.5))


def in_real_form(matrix):
    return np.block([[matrix.real, matrix.imag], [-matrix.imag, matrix.real]])


def two_halves(matrix):
    high = matrix.astype(ml_dtypes.bfloat16)
    low = (matrix - high.astype(np.float64)).astype(ml_dtypes.bfloat16)
    return high, low


def make_tables():
    steps = np.arange(NV)
    whole = np.exp(-2j * np.pi * (steps[:, None] * steps[None, :] % NV) / NV)
    four = np.arange(4)
    quarter = np.exp(-2j * np.pi * (four[:, None] * four[None, :] % 4) / 4)
    lanes = np.kron(quarter, whole)
    slots = np.kron(np.eye(4), whole)
    blocks = [
        in_real_form(lanes),
        in_real_form(slots),
        in_real_form(slots.conj() / NV),
        in_real_form(lanes.conj() / NV**2),
    ]
    rows = []
    for block in blocks:
        rows.extend(two_halves(block))
    back = whole.conj() / NV
    for left in (
        np.concatenate([whole.real, whole.imag], axis=0),
        np.concatenate([back.real, -back.imag], axis=1),
    ):
        high, low = two_halves(left)
        wide = np.concatenate([high, high, low], axis=1)
        rows.append(np.pad(wide, ((0, 0), (0, 256 - wide.shape[1]))))
    return np.concatenate(rows, axis=0)


def make_twiddles():
    angle = -2.0 * np.pi * (np.arange(8)[:, None] * (np.arange(128)[None, :] // 32)) / NV
    parts = np.stack([np.cos(angle), np.sin(angle)], axis=1).astype(np.float32)
    return np.broadcast_to(parts[:, :, None, :], (8, 2, 8, 128)).reshape(128, 128).copy()


ROWS_OF = {
    "lanes": (0, 256),
    "slots": (512, 768),
    "slots_back": (1024, 1280),
    "lanes_back": (1536, 1792),
}
LEFT_ROW = 2048
LEFT_BACK_ROW = 2112
TABLE_ROWS = 2144


def split(x):
    high = x.astype(jnp.bfloat16)
    low = (x - high.astype(jnp.float32)).astype(jnp.bfloat16)
    return high, low


def dot(a, b):
    return jnp.dot(a, b, preferred_element_type=jnp.float32)


def product(x, high, low):
    xh, xl = split(x)
    return dot(
        jnp.concatenate([xh, xl, xh], axis=1), jnp.concatenate([high, high, low], axis=0)
    )


def left_product(left, x):
    xh, xl = split(x)
    return dot(left, jnp.concatenate([xh, xl, xh], axis=0))


def turned(x):
    return jnp.concatenate([x[:, :128].T, x[:, 128:].T], axis=1)


def turn_by(value, factor):
    re, im = value
    fr, fi = factor
    return (re * fr - im * fi, re * fi + im * fr)


def plus(a, b):
    return (a[0] + b[0], a[1] + b[1])


def minus(a, b):
    return (a[0] - b[0], a[1] - b[1])


def four_points(x, sign):
    s0, d0 = plus(x[0], x[2]), minus(x[0], x[2])
    s1, d1 = plus(x[1], x[3]), minus(x[1], x[3])
    side = (-sign * d1[1], sign * d1[0]) if sign > 0 else (d1[1], -d1[0])
    return [plus(s0, s1), plus(d0, side), minus(s0, s1), minus(d0, side)]


def eight_points(x, sign):
    even = four_points(x[0::2], sign)
    odd = four_points(x[1::2], sign)
    o1, o2, o3 = odd[1], odd[2], odd[3]
    if sign < 0:
        o1 = ((o1[0] + o1[1]) * ROOT_HALF, (o1[1] - o1[0]) * ROOT_HALF)
        o2 = (o2[1], -o2[0])
        o3 = ((o3[1] - o3[0]) * ROOT_HALF, (o3[0] + o3[1]) * -ROOT_HALF)
    else:
        o1 = ((o1[0] - o1[1]) * ROOT_HALF, (o1[1] + o1[0]) * ROOT_HALF)
        o2 = (-o2[1], o2[0])
        o3 = ((o3[0] + o3[1]) * -ROOT_HALF, (o3[0] - o3[1]) * ROOT_HALF)
    odd = [odd[0], o1, o2, o3]
    return [plus(e, o) for e, o in zip(even, odd)] + [minus(e, o) for e, o in zip(even, odd)]


def forward_eight(x, factors):
    turned_x = [x[0]] + [turn_by(v, f) for v, f in zip(x[1:], factors)]
    return eight_points(turned_x, -1)


def backward_eight(x, factors):
    y = eight_points(x, 1)
    return [y[0]] + [turn_by(v, (fr, -fi)) for v, (fr, fi) in zip(y[1:], factors)]


def exchange_lanes(tiles):
    group = lax.broadcasted_iota(jnp.int32, (8, 128), 1) // 32
    upper = group >= 2
    odd = group % 2 == 1
    y = [None] * 4
    for h in range(2):
        y[h] = jnp.where(upper, pltpu.roll(tiles[h + 2], 64, 1), tiles[h])
        y[h + 2] = jnp.where(upper, tiles[h + 2], pltpu.roll(tiles[h], 64, 1))
    z = [None] * 4
    for h in (0, 2):
        z[h] = jnp.where(odd, pltpu.roll(y[h + 1], 32, 1), y[h])
        z[h + 1] = jnp.where(odd, y[h + 1], pltpu.roll(y[h], 96, 1))
    return z


def kernel(
    adjoint_hbm,
    state_hbm,
    gain_left,
    gain_right,
    table_hbm,
    twiddle_hbm,
    out,
    table,
    twiddles,
    adjoint,
    state,
    beside,
    passed_own,
    state_sent,
    passed_sent,
    state_all,
    passed_all,
    result,
    arrived,
    raw,
    gains,
    upper,
    loss_gain,
    loss_upper,
    spectrum,
    product_spectrum,
    total,
    loss,
    work,
    local_sem,
    halo_sem,
    state_send,
    state_recv,
    passed_send,
    passed_recv,
    result_send,
    result_recv,
    gain_send,
    gain_recv,
    share_send,
    share_recv,
    loss_send,
    loss_recv,
    near_here,
    far_here,
):
    tile = lax.axis_index("tile")
    quad = lax.axis_index("quad")
    tiles = lax.axis_size("tile")
    column = lax.rem(quad, 4)
    row = quad // 4
    core = lax.rem(tile, 2)
    sibling = tile + 1 - 2 * core
    partner_tile = lax.rem(tile + tiles // 2, tiles)
    ahead = quad >= 8
    up, down = lax.rem(tile + 1, tiles), lax.rem(tile + tiles - 1, tiles)
    source_tile = jnp.where(ahead, up, down)
    target_tile = jnp.where(ahead, down, up)

    barrier = pltpu.get_barrier_semaphore()
    even_tile = tile - core
    far_listener = partner_tile - core + 1
    for over, across in FARTHEST_FIRST:
        peer = lax.rem(row + over, 4) * 4 + lax.rem(column + across, 4)
        pl.semaphore_signal(
            barrier, inc=1, device_id={"tile": far_listener, "quad": peer}, device_id_type=MESH
        )
    for step in (2, 1, 3):
        peer = row * 4 + lax.rem(column + step, 4)
        pl.semaphore_signal(
            barrier, inc=1, device_id={"tile": even_tile, "quad": peer}, device_id_type=MESH
        )
    near_source = source_tile - lax.rem(source_tile, 2)

    @pl.when(near_source != tile)
    def _():
        pl.semaphore_signal(barrier, inc=1, device_id={"tile": near_source}, device_id_type=MESH)

    @pl.when(core == 1)
    def _():
        pl.semaphore_signal(barrier, inc=1, device_id={"tile": sibling}, device_id_type=MESH)

    fetch_twiddles = pltpu.make_async_copy(twiddle_hbm, twiddles, local_sem.at[5])
    fetch_table = pltpu.make_async_copy(table_hbm, table, local_sem.at[0])
    fetch_left = pltpu.make_async_copy(gain_left.at[0], raw.at[0], local_sem.at[1])
    fetch_right = pltpu.make_async_copy(gain_right.at[0], raw.at[1], local_sem.at[2])
    fetch_state = pltpu.make_async_copy(state_hbm, state, local_sem.at[3])
    fetch_adjoint = pltpu.make_async_copy(adjoint_hbm, adjoint, local_sem.at[4])
    fetch_state.start()
    fetch_adjoint.start()
    fetch_left.start()
    fetch_right.start()
    fetch_table.start()
    fetch_twiddles.start()

    fetch_left.wait()
    fetch_right.wait()
    lane = lax.broadcasted_iota(jnp.int32, (8, 128), 1)
    line = lax.broadcasted_iota(jnp.int32, (8, 128), 0)
    mirror_lane = lax.rem(4 - lane // 32, 4) * 32 + lax.rem(32 - lax.rem(lane, 32), 32)
    mirror_line = lax.rem(8 - line, 8)

    def mirrored(tile_of, h, r):
        def column(n):
            return jnp.where(lane < 32, tile_of((8 - h) % 8, n), tile_of((7 - h) % 8, n))

        rest = jnp.take_along_axis(column(3 - r), mirror_line, axis=0)
        both = jnp.where(line == 0, column((4 - r) % 4), rest)
        return jnp.take_along_axis(both, mirror_lane, axis=1)

    def raw_tile(kind):
        return lambda h, r: raw[kind, 8 * r : 8 * r + 8, 128 * h : 128 * h + 128]

    own_rows = column * 32
    for h in range(5):
        for r in range(4):
            at = pl.ds(own_rows + 8 * r, 8)
            here = slice(128 * h, 128 * h + 128)
            left, right = raw_tile(0)(h, r), raw_tile(1)(h, r)
            left_m, right_m = mirrored(raw_tile(0), h, r), mirrored(raw_tile(1), h, r)
            gains[0, at, here] = (left + left_m) * 0.5
            gains[1, at, here] = (right + right_m) * 0.5
            gains[2, at, here] = (left * right + left_m * right_m) * 0.5

    fetch_state.wait()
    for j in range(2):
        cells = exchange_lanes([state[j, 8 * h : 8 * h + 8, :] for h in range(4)])
        for cell in range(4):
            state_sent[cell, 8 * j : 8 * j + 8, :] = cells[cell]

    @pl.when(core == 0)
    def _():
        pl.semaphore_wait(barrier, jnp.where(ahead, 8, 9))
        pl.semaphore_signal(near_here, inc=1, device_id={"tile": sibling}, device_id_type=MESH)

    @pl.when(core == 1)
    def _():
        pl.semaphore_wait(near_here, 1)

    halo = pltpu.make_async_remote_copy(
        src_ref=adjoint,
        dst_ref=beside,
        send_sem=halo_sem.at[0],
        recv_sem=halo_sem.at[1],
        device_id={"tile": target_tile},
        device_id_type=MESH,
    )
    fetch_adjoint.wait()
    halo.start()

    def to_peer(sent, whole, send, recv, peer):
        return pltpu.make_async_remote_copy(
            src_ref=sent.at[lax.rem(peer, 4)],
            dst_ref=whole.at[pl.ds(quad * 16, 16), :],
            send_sem=send,
            recv_sem=recv,
            device_id={"tile": partner_tile, "quad": peer},
            device_id_type=MESH,
        )

    def all_of(whole, send, recv):
        return pltpu.make_async_remote_copy(
            src_ref=whole,
            dst_ref=whole,
            send_sem=send,
            recv_sem=recv,
            device_id={"tile": partner_tile},
            device_id_type=MESH,
        )

    def for_peers(action):
        for over, across in FARTHEST_FIRST:
            action(lax.rem(row + over, 4) * 4 + lax.rem(column + across, 4))

    state_refs = (state_sent, state_all, state_send, state_recv)
    passed_refs = (passed_sent, passed_all, passed_send, passed_recv)

    def gain_copy(kind, send, recv, position):
        return pltpu.make_async_remote_copy(
            src_ref=gains.at[kind, pl.ds(column * 32, 32), :],
            dst_ref=gains.at[kind, pl.ds(column * 32, 32), :],
            send_sem=send.at[position],
            recv_sem=recv.at[column],
            device_id={"quad": row * 4 + position},
            device_id_type=MESH,
        )

    def gain_arrival(position, kind, send, recv):
        return pltpu.make_async_remote_copy(
            src_ref=gains.at[kind, pl.ds(position * 32, 32), :],
            dst_ref=gains.at[kind, pl.ds(position * 32, 32), :],
            send_sem=send.at[position],
            recv_sem=recv.at[position],
            device_id={"tile": sibling},
            device_id_type=MESH,
        )

    beside_columns = [lax.rem(column + step, 4) for step in (2, 1, 3)]
    for position in beside_columns:
        gain_copy(core, gain_send, gain_recv, position).start()

    @pl.when(core == 1)
    def _():
        pl.semaphore_wait(barrier, 32)
        pl.semaphore_signal(far_here, inc=1, device_id={"tile": sibling}, device_id_type=MESH)

    @pl.when(core == 0)
    def _():
        pl.semaphore_wait(far_here, 1)

    for_peers(lambda peer: to_peer(*state_refs, peer).start())

    halo.wait_recv()
    lower = lane < 64
    odd_cell = lane // 32 % 2 == 1
    from_own = jnp.logical_xor(lower, jnp.logical_not(ahead))
    for j in range(2):
        plane = (quad * 2 + j).astype(jnp.float32)
        speed_x = jnp.abs((plane - (NV - 1) / 2.0) / NV)
        for h in range(4):
            rows = slice(8 * h, 8 * h + 8)
            own = adjoint[j, rows, :]
            second = beside[j, rows, :]
            first = jnp.where(from_own, pltpu.roll(own, 64, 1), pltpu.roll(second, 64, 1))
            partner = jnp.where(odd_cell, pltpu.roll(own, 32, 1), pltpu.roll(own, 96, 1))
            b = (lax.broadcasted_iota(jnp.int32, (8, 128), 0) + 8 * h).astype(jnp.float32)
            speed_y = jnp.abs((b - (NV - 1) / 2.0) / NV)
            passed_own[j, rows, :] = (
                own
                - speed_x * (3.0 * own - 4.0 * first + second) * 0.5
                - 2.0 * speed_y * (own - partner)
            )
        cells = exchange_lanes([passed_own[j, 8 * h : 8 * h + 8, :] for h in range(4)])
        for cell in range(4):
            passed_sent[cell, 8 * j : 8 * j + 8, :] = cells[cell]
    for_peers(lambda peer: to_peer(*passed_refs, peer).start())

    def tables(name):
        high, low = ROWS_OF[name]
        return table[high : high + 256, :], table[low : low + 256, :]

    def plane_of(ref, low_index):
        return ref[pl.ds(low_index, 32, stride=8), :]

    def tile_at(n):
        return slice(128 * n, 128 * n + 128)

    def factors():
        at = [slice(8 * n, 8 * n + 8) for n in range(16)]
        return [(twiddles[at[2 * n], :], twiddles[at[2 * n + 1], :]) for n in range(1, 8)]

    def load_eight(ref, rows):
        return [(ref[n, rows, :128], ref[n, rows, 128:]) for n in range(8)]

    def store_eight(ref, rows, values):
        for n, (re, im) in enumerate(values):
            ref[n, rows, :128] = re
            ref[n, rows, 128:] = im

    def eight_rows(start):
        return pl.ds(pl.multiple_of(start, 8), 8)

    def transform(planes, ref):
        left = table[LEFT_ROW : LEFT_ROW + 64, :96]
        mid = left_product(left, jnp.concatenate(planes, axis=1))
        rows = [
            jnp.concatenate([mid[:32, tile_at(n)], mid[32:, tile_at(n)]], axis=1) for n in range(8)
        ]
        ref[...] = product(jnp.concatenate(rows, axis=0), *tables("lanes")).reshape(8, NV, 256)

        def finish(r, carry):
            rows = eight_rows(8 * r)
            store_eight(ref, rows, forward_eight(load_eight(ref, rows), factors()))
            return carry

        lax.fori_loop(0, 4, finish, 0)

    def unfold(kind):
        def body(pair, carry):
            def tile_of(h, r):
                return gains[kind, eight_rows(pair * 32 + 8 * r), tile_at(h)]

            for h in (7, 6, 5, 4):
                for r in range(4):
                    values = mirrored(tile_of, h, r)
                    if h == 4:
                        values = jnp.where(lane < 32, tile_of(4, r), values)
                    upper[kind, eight_rows(pair * 32 + 8 * r), tile_at(h - 4)] = values
            return carry

        lax.fori_loop(0, 4, body, 0)

    for position in beside_columns:
        gain_arrival(position, core, gain_send, gain_recv).wait_recv()
        gain_arrival(position, core, share_send, share_recv).start()
    for position in beside_columns:
        gain_copy(2, loss_send, loss_recv, position).start()
    unfold(core)

    fetch_table.wait()
    fetch_twiddles.wait()
    all_of(*state_refs[1:]).wait_recv()
    transform([plane_of(state_all, n) for n in range(8)], spectrum)


    def wait_passed():
        all_of(*passed_refs[1:]).wait_recv()

    def transform_product():
        planes = [plane_of(state_all, n) * plane_of(passed_all, n) for n in range(8)]
        transform(planes, product_spectrum)

    wait_passed()
    transform_product()

    for position in beside_columns:
        gain_arrival(position, 1 - core, share_send, share_recv).wait_recv()
    unfold(1 - core)

    def gain_tile(kind, rows, n):
        return gains[kind, rows, tile_at(n)] if n < 4 else upper[kind, rows, tile_at(n - 4)]

    def filter_step(r, carry):
        rows = eight_rows(8 * r)
        both = []
        for n, (re, im) in enumerate(load_eight(spectrum, eight_rows(8 * lax.rem(r, 4)))):
            left, right = gain_tile(0, rows, n), gain_tile(1, rows, n)
            both.append((left * re - right * im, left * im + right * re))
        store_eight(work, rows, backward_eight(both, factors()))
        return carry

    lax.fori_loop(0, 16, filter_step, 0)

    def all_turned(values):
        parts = [turned(values[tile_at(n)]) for n in range(values.shape[0] // 128)]
        return jnp.concatenate(parts, axis=0)

    for i in range(0, 8, BLOCK):
        half = product(work[i : i + BLOCK].reshape(BLOCK * 128, 256), *tables("lanes_back"))
        fields = product(all_turned(half), *tables("slots_back"))
        work[i : i + BLOCK] = fields.reshape(BLOCK, 128, 256)

    for i in range(0, 8, BLOCK):
        crossed = []
        for n in range(i, i + BLOCK):
            weights = jnp.concatenate([plane_of(passed_all, n)] * 4, axis=0).T
            fields = work[n]
            crossed.append(
                jnp.concatenate([fields[:, 128:] * weights, fields[:, :128] * weights], axis=1)
            )
        half = product(jnp.concatenate(crossed, axis=0), *tables("slots"))
        fields = product(all_turned(half), *tables("lanes"))
        work[i : i + BLOCK] = fields.reshape(BLOCK, 128, 256)

    for position in beside_columns:
        gain_arrival(position, 2, loss_send, loss_recv).wait_recv()

    def loss_tile(h, r):
        return loss_gain[8 * r : 8 * r + 8, tile_at(h)]

    for r in range(4):
        for h in range(5):
            starts = [32 * pair + 8 * r for pair in range(4)]
            b = [gains[2, start : start + 8, tile_at(h)] for start in starts]
            loss_gain[8 * r : 8 * r + 8, tile_at(h)] = (b[0] + b[1]) + (b[2] + b[3])
    for h in (7, 6, 5, 4):
        for r in range(4):
            values = mirrored(loss_tile, h, r)
            if h == 4:
                values = jnp.where(lane < 32, loss_tile(4, r), values)
            loss_upper[8 * r : 8 * r + 8, tile_at(h - 4)] = values

    def total_step(r, carry):
        rows = eight_rows(8 * r)
        sums = []
        weights = [loss_gain[rows, tile_at(n)] for n in range(4)]
        weights += [loss_upper[rows, tile_at(n)] for n in range(4)]
        for n, (re, im) in enumerate(load_eight(product_spectrum, rows)):
            sums.append((-weights[n] * re, -weights[n] * im))
        for pair in range(4):
            at = eight_rows(32 * pair + 8 * r)
            for n, (re, im) in enumerate(forward_eight(load_eight(work, at), factors())):
                left, right = gain_tile(0, at, n), gain_tile(1, at, n)
                sums[n] = (
                    sums[n][0] + (left * re + right * im),
                    sums[n][1] + (left * im - right * re),
                )
        store_eight(total, rows, backward_eight(sums, factors()))
        lost = [
            (weights[n] * re, weights[n] * im)
            for n, (re, im) in enumerate(load_eight(spectrum, rows))
        ]
        store_eight(loss, rows, backward_eight(lost, factors()))
        return carry

    lax.fori_loop(0, 4, total_step, 0)

    both = jnp.concatenate([total[...].reshape(256, 256), loss[...].reshape(256, 256)], axis=0)
    both = product(both, *tables("lanes_back"))

    def last_axis(values):
        parts = [values[32 * n : 32 * n + 32] for n in range(8)]
        re = jnp.concatenate([part[:, :128] for part in parts], axis=1)
        im = jnp.concatenate([part[:, 128:] for part in parts], axis=1)
        left = table[LEFT_BACK_ROW : LEFT_BACK_ROW + 32, :192]
        return left_product(left, jnp.concatenate([re, im], axis=0))

    gained, lost = last_axis(both[:256]), last_axis(both[256:])
    for n in range(8):
        value = gained[:, tile_at(n)] - plane_of(passed_all, n) * lost[:, tile_at(n)]
        result[pl.ds(n, 32, stride=8), :] = value

    def result_copy(peer):
        return pltpu.make_async_remote_copy(
            src_ref=result.at[pl.ds(peer * 16, 16), :],
            dst_ref=arrived.at[pl.ds(quad * 16, 16), :],
            send_sem=result_send,
            recv_sem=result_recv,
            device_id={"tile": partner_tile, "quad": peer},
            device_id_type=MESH,
        )

    for_peers(lambda peer: result_copy(peer).start())

    halo.wait_send()
    all_of(*state_refs[1:]).wait_send()
    all_of(*passed_refs[1:]).wait_send()
    for position in beside_columns:
        gain_copy(core, gain_send, gain_recv, position).wait_send()
        gain_copy(2, loss_send, loss_recv, position).wait_send()
        gain_arrival(position, core, share_send, share_recv).wait_send()

    all_of(arrived, result_send, result_recv).wait_recv()

    def arrived_at(source, j):
        return arrived[16 * source + 8 * j : 16 * source + 8 * j + 8, :]

    for j in range(2):
        cells = [
            (arrived_at(cell, j) + arrived_at(4 + cell, j))
            + (arrived_at(8 + cell, j) + arrived_at(12 + cell, j))
            for cell in range(4)
        ]
        parts = exchange_lanes(cells)
        for h in range(4):
            part = slice(8 * h, 8 * h + 8)
            out[j, part, :] = passed_own[j, part, :] + parts[h] * (1.0 / 16.0)

    all_of(arrived, result_send, result_recv).wait_send()


def local(adjoint_next, saved_state, gain_left, gain_right):
    share = adjoint_next.shape
    whole_field = pltpu.VMEM((8, 128, 256), jnp.float32)
    one_field = pltpu.VMEM((8, NV, 256), jnp.float32)
    dma = pltpu.SemaphoreType.DMA
    in_vmem = pl.BlockSpec(memory_space=pltpu.VMEM)
    anywhere = pl.BlockSpec(memory_space=pl.ANY)
    table = jnp.asarray(make_tables())
    return pl.pallas_call(
        kernel,
        out_shape=jax.ShapeDtypeStruct(share, jnp.float32),
        in_specs=[anywhere] * 6,
        out_specs=in_vmem,
        scratch_shapes=[
            pltpu.VMEM((TABLE_ROWS, 256), jnp.bfloat16),
            pltpu.VMEM((128, 128), jnp.float32),
            pltpu.VMEM(share, jnp.float32),
            pltpu.VMEM(share, jnp.float32),
            pltpu.VMEM(share, jnp.float32),
            pltpu.VMEM(share, jnp.float32),
            pltpu.VMEM((4, 16, 128), jnp.float32),
            pltpu.VMEM((4, 16, 128), jnp.float32),
            pltpu.VMEM((256, 128), jnp.float32),
            pltpu.VMEM((256, 128), jnp.float32),
            pltpu.VMEM((256, 128), jnp.float32),
            pltpu.VMEM((256, 128), jnp.float32),
            pltpu.VMEM((2, NV, 1024), jnp.float32),
            pltpu.VMEM((3, 128, HALF), jnp.float32),
            pltpu.VMEM((2, 128, 512), jnp.float32),
            pltpu.VMEM((NV, HALF), jnp.float32),
            pltpu.VMEM((NV, 512), jnp.float32),
            one_field,
            one_field,
            one_field,
            one_field,
            whole_field,
            dma((6,)),
            dma((2,)),
            dma,
            dma,
            dma,
            dma,
            dma,
            dma,
            dma((4,)),
            dma((4,)),
            dma((4,)),
            dma((4,)),
            dma((4,)),
            dma((4,)),
            pltpu.SemaphoreType.REGULAR,
            pltpu.SemaphoreType.REGULAR,
        ],
        compiler_params=pltpu.CompilerParams(
            collective_id=0, has_side_effects=True, vmem_limit_bytes=60 * 1024 * 1024
        ),
        name="adjoint_step",
    )(adjoint_next, saved_state, gain_left, gain_right, table, jnp.asarray(make_twiddles()))


def solution(mesh):
    in_specs = (
        P("quad", None, "tile"),
        P("quad", None, "tile"),
        P("quad", None, None),
        P("quad", None, None),
    )
    out_specs = P("quad", None, "tile")
    return jax.shard_map(local, mesh=mesh, in_specs=in_specs, out_specs=out_specs, check_vma=False)
```

```python
import functools
import ml_dtypes
import numpy as np
import jax
import jax.numpy as jnp
from jax import lax
from jax.experimental import pallas as pl
from jax.experimental.pallas import tpu as pltpu
from jax.sharding import PartitionSpec as P

MESH = pl.DeviceIdType.MESH
NV = 32
BLOCK = 2
FARTHEST_FIRST = sorted(
    ((over, across) for over in range(4) for across in range(4)),
    key=lambda step: -(2 * min(step[0], 4 - step[0]) + min(step[1], 4 - step[1])),
)
HALF = 640
ROOT_HALF = float(np.sqrt(0.5))


def in_real_form(matrix):
    return np.block([[matrix.real, matrix.imag], [-matrix.imag, matrix.real]])


def two_halves(matrix):
    high = matrix.astype(ml_dtypes.bfloat16)
    low = (matrix - high.astype(np.float64)).astype(ml_dtypes.bfloat16)
    return high, low


def make_tables():
    steps = np.arange(NV)
    whole = np.exp(-2j * np.pi * (steps[:, None] * steps[None, :] % NV) / NV)
    four = np.arange(4)
    quarter = np.exp(-2j * np.pi * (four[:, None] * four[None, :] % 4) / 4)
    lanes = np.kron(quarter, whole)
    slots = np.kron(np.eye(4), whole)
    blocks = [
        in_real_form(lanes),
        in_real_form(slots),
        in_real_form(slots.conj() / NV),
        in_real_form(lanes.conj() / NV**2),
    ]
    rows = []
    for block in blocks:
        rows.extend(two_halves(block))
    back = whole.conj() / NV
    for left in (
        np.concatenate([whole.real, whole.imag], axis=0),
        np.concatenate([back.real, -back.imag], axis=1),
    ):
        high, low = two_halves(left)
        wide = np.concatenate([high, high, low], axis=1)
        rows.append(np.pad(wide, ((0, 0), (0, 256 - wide.shape[1]))))
    return np.concatenate(rows, axis=0)


def make_twiddles():
    angle = -2.0 * np.pi * (np.arange(8)[:, None] * (np.arange(128)[None, :] // 32)) / NV
    parts = np.stack([np.cos(angle), np.sin(angle)], axis=1).astype(np.float32)
    return np.broadcast_to(parts[:, :, None, :], (8, 2, 8, 128)).reshape(128, 128).copy()


ROWS_OF = {
    "lanes": (0, 256),
    "slots": (512, 768),
    "slots_back": (1024, 1280),
    "lanes_back": (1536, 1792),
}
LEFT_ROW = 2048
LEFT_BACK_ROW = 2112
TABLE_ROWS = 2144


def split(x):
    high = x.astype(jnp.bfloat16)
    low = (x - high.astype(jnp.float32)).astype(jnp.bfloat16)
    return high, low


def dot(a, b):
    return jnp.dot(a, b, preferred_element_type=jnp.float32)


def product(x, high, low):
    xh, xl = split(x)
    return dot(
        jnp.concatenate([xh, xl, xh], axis=1), jnp.concatenate([high, high, low], axis=0)
    )


def left_product(left, x):
    xh, xl = split(x)
    return dot(left, jnp.concatenate([xh, xl, xh], axis=0))


def turned(x):
    return jnp.concatenate([x[:, :128].T, x[:, 128:].T], axis=1)


def turn_by(value, factor):
    re, im = value
    fr, fi = factor
    return (re * fr - im * fi, re * fi + im * fr)


def plus(a, b):
    return (a[0] + b[0], a[1] + b[1])


def minus(a, b):
    return (a[0] - b[0], a[1] - b[1])


def four_points(x, sign):
    s0, d0 = plus(x[0], x[2]), minus(x[0], x[2])
    s1, d1 = plus(x[1], x[3]), minus(x[1], x[3])
    side = (-sign * d1[1], sign * d1[0]) if sign > 0 else (d1[1], -d1[0])
    return [plus(s0, s1), plus(d0, side), minus(s0, s1), minus(d0, side)]


def eight_points(x, sign):
    even = four_points(x[0::2], sign)
    odd = four_points(x[1::2], sign)
    o1, o2, o3 = odd[1], odd[2], odd[3]
    if sign < 0:
        o1 = ((o1[0] + o1[1]) * ROOT_HALF, (o1[1] - o1[0]) * ROOT_HALF)
        o2 = (o2[1], -o2[0])
        o3 = ((o3[1] - o3[0]) * ROOT_HALF, (o3[0] + o3[1]) * -ROOT_HALF)
    else:
        o1 = ((o1[0] - o1[1]) * ROOT_HALF, (o1[1] + o1[0]) * ROOT_HALF)
        o2 = (-o2[1], o2[0])
        o3 = ((o3[0] + o3[1]) * -ROOT_HALF, (o3[0] - o3[1]) * ROOT_HALF)
    odd = [odd[0], o1, o2, o3]
    return [plus(e, o) for e, o in zip(even, odd)] + [minus(e, o) for e, o in zip(even, odd)]


def forward_eight(x, factors):
    turned_x = [x[0]] + [turn_by(v, f) for v, f in zip(x[1:], factors)]
    return eight_points(turned_x, -1)


def backward_eight(x, factors):
    y = eight_points(x, 1)
    return [y[0]] + [turn_by(v, (fr, -fi)) for v, (fr, fi) in zip(y[1:], factors)]


def exchange_lanes(tiles):
    group = lax.broadcasted_iota(jnp.int32, (8, 128), 1) // 32
    upper = group >= 2
    odd = group % 2 == 1
    y = [None] * 4
    for h in range(2):
        y[h] = jnp.where(upper, pltpu.roll(tiles[h + 2], 64, 1), tiles[h])
        y[h + 2] = jnp.where(upper, tiles[h + 2], pltpu.roll(tiles[h], 64, 1))
    z = [None] * 4
    for h in (0, 2):
        z[h] = jnp.where(odd, pltpu.roll(y[h + 1], 32, 1), y[h])
        z[h + 1] = jnp.where(odd, y[h + 1], pltpu.roll(y[h], 96, 1))
    return z


def kernel(
    adjoint_hbm,
    state_hbm,
    gain_left,
    gain_right,
    table_hbm,
    twiddle_hbm,
    out,
    table,
    twiddles,
    adjoint,
    state,
    beside,
    passed_own,
    state_sent,
    passed_sent,
    state_all,
    passed_all,
    result,
    arrived,
    raw,
    gains,
    upper,
    loss_gain,
    loss_upper,
    spectrum,
    product_spectrum,
    total,
    loss,
    work,
    local_sem,
    halo_sem,
    state_send,
    state_recv,
    passed_send,
    passed_recv,
    result_send,
    result_recv,
    gain_send,
    gain_recv,
    share_send,
    share_recv,
    loss_send,
    loss_recv,
    near_here,
    far_here,
):
    tile = lax.axis_index("tile")
    quad = lax.axis_index("quad")
    tiles = lax.axis_size("tile")
    column = lax.rem(quad, 4)
    row = quad // 4
    core = lax.rem(tile, 2)
    sibling = tile + 1 - 2 * core
    partner_tile = lax.rem(tile + tiles // 2, tiles)
    ahead = quad >= 8
    up, down = lax.rem(tile + 1, tiles), lax.rem(tile + tiles - 1, tiles)
    source_tile = jnp.where(ahead, up, down)
    target_tile = jnp.where(ahead, down, up)

    barrier = pltpu.get_barrier_semaphore()
    even_tile = tile - core
    far_listener = partner_tile - core + 1
    for step in (2, 1, 3):
        peer = row * 4 + lax.rem(column + step, 4)
        pl.semaphore_signal(
            barrier, inc=1, device_id={"tile": even_tile, "quad": peer}, device_id_type=MESH
        )
    near_source = source_tile - lax.rem(source_tile, 2)

    @pl.when(near_source != tile)
    def _():
        pl.semaphore_signal(barrier, inc=1, device_id={"tile": near_source}, device_id_type=MESH)

    @pl.when(core == 1)
    def _():
        pl.semaphore_signal(barrier, inc=1, device_id={"tile": sibling}, device_id_type=MESH)

    for over, across in FARTHEST_FIRST:
        peer = lax.rem(row + over, 4) * 4 + lax.rem(column + across, 4)
        pl.semaphore_signal(
            barrier, inc=1, device_id={"tile": far_listener, "quad": peer}, device_id_type=MESH
        )

    fetch_twiddles = pltpu.make_async_copy(twiddle_hbm, twiddles, local_sem.at[5])
    fetch_table = pltpu.make_async_copy(table_hbm, table, local_sem.at[0])
    fetch_left = pltpu.make_async_copy(gain_left.at[0], raw.at[0], local_sem.at[1])
    fetch_right = pltpu.make_async_copy(gain_right.at[0], raw.at[1], local_sem.at[2])
    fetch_state = pltpu.make_async_copy(state_hbm, state, local_sem.at[3])
    fetch_adjoint = pltpu.make_async_copy(adjoint_hbm, adjoint, local_sem.at[4])
    fetch_state.start()
    fetch_adjoint.start()
    fetch_left.start()
    fetch_right.start()
    fetch_table.start()
    fetch_twiddles.start()

    fetch_left.wait()
    fetch_right.wait()
    lane = lax.broadcasted_iota(jnp.int32, (8, 128), 1)
    line = lax.broadcasted_iota(jnp.int32, (8, 128), 0)
    mirror_lane = lax.rem(4 - lane // 32, 4) * 32 + lax.rem(32 - lax.rem(lane, 32), 32)
    mirror_line = lax.rem(8 - line, 8)

    def mirrored(tile_of, h, r):
        def column(n):
            return jnp.where(lane < 32, tile_of((8 - h) % 8, n), tile_of((7 - h) % 8, n))

        rest = jnp.take_along_axis(column(3 - r), mirror_line, axis=0)
        both = jnp.where(line == 0, column((4 - r) % 4), rest)
        return jnp.take_along_axis(both, mirror_lane, axis=1)

    def raw_tile(kind):
        return lambda h, r: raw[kind, 8 * r : 8 * r + 8, 128 * h : 128 * h + 128]

    own_rows = column * 32

    def fold(kind):
        for h in range(5):
            for r in range(4):
                at, here = pl.ds(own_rows + 8 * r, 8), slice(128 * h, 128 * h + 128)
                value = raw_tile(kind)(h, r) + mirrored(raw_tile(kind), h, r)
                gains[kind, at, here] = value * 0.5

    def fold_loss():
        for h in range(5):
            for r in range(4):
                at, here = pl.ds(own_rows + 8 * r, 8), slice(128 * h, 128 * h + 128)
                direct = raw_tile(0)(h, r) * raw_tile(1)(h, r)
                other = mirrored(raw_tile(0), h, r) * mirrored(raw_tile(1), h, r)
                gains[2, at, here] = (direct + other) * 0.5

    fold(core)

    fetch_state.wait()
    for j in range(2):
        cells = exchange_lanes([state[j, 8 * h : 8 * h + 8, :] for h in range(4)])
        for cell in range(4):
            state_sent[cell, 8 * j : 8 * j + 8, :] = cells[cell]

    @pl.when(core == 0)
    def _():
        pl.semaphore_wait(barrier, jnp.where(ahead, 8, 9))
        pl.semaphore_signal(near_here, inc=1, device_id={"tile": sibling}, device_id_type=MESH)

    @pl.when(core == 1)
    def _():
        pl.semaphore_wait(near_here, 1)

    halo = pltpu.make_async_remote_copy(
        src_ref=adjoint,
        dst_ref=beside,
        send_sem=halo_sem.at[0],
        recv_sem=halo_sem.at[1],
        device_id={"tile": target_tile},
        device_id_type=MESH,
    )
    fetch_adjoint.wait()
    halo.start()

    def to_peer(sent, whole, send, recv, peer):
        return pltpu.make_async_remote_copy(
            src_ref=sent.at[lax.rem(peer, 4)],
            dst_ref=whole.at[pl.ds(quad * 16, 16), :],
            send_sem=send,
            recv_sem=recv,
            device_id={"tile": partner_tile, "quad": peer},
            device_id_type=MESH,
        )

    def all_of(whole, send, recv):
        return pltpu.make_async_remote_copy(
            src_ref=whole,
            dst_ref=whole,
            send_sem=send,
            recv_sem=recv,
            device_id={"tile": partner_tile},
            device_id_type=MESH,
        )

    def for_peers(action):
        for over, across in FARTHEST_FIRST:
            action(lax.rem(row + over, 4) * 4 + lax.rem(column + across, 4))

    state_refs = (state_sent, state_all, state_send, state_recv)
    passed_refs = (passed_sent, passed_all, passed_send, passed_recv)

    def gain_copy(kind, send, recv, position):
        return pltpu.make_async_remote_copy(
            src_ref=gains.at[kind, pl.ds(column * 32, 32), :],
            dst_ref=gains.at[kind, pl.ds(column * 32, 32), :],
            send_sem=send.at[position],
            recv_sem=recv.at[column],
            device_id={"quad": row * 4 + position},
            device_id_type=MESH,
        )

    def gain_arrival(position, kind, send, recv):
        return pltpu.make_async_remote_copy(
            src_ref=gains.at[kind, pl.ds(position * 32, 32), :],
            dst_ref=gains.at[kind, pl.ds(position * 32, 32), :],
            send_sem=send.at[position],
            recv_sem=recv.at[position],
            device_id={"tile": sibling},
            device_id_type=MESH,
        )

    beside_columns = [lax.rem(column + step, 4) for step in (2, 1, 3)]
    for position in beside_columns:
        gain_copy(core, gain_send, gain_recv, position).start()

    @pl.when(core == 1)
    def _():
        pl.semaphore_wait(barrier, 32)
        pl.semaphore_signal(far_here, inc=1, device_id={"tile": sibling}, device_id_type=MESH)

    @pl.when(core == 0)
    def _():
        pl.semaphore_wait(far_here, 1)

    for_peers(lambda peer: to_peer(*state_refs, peer).start())

    halo.wait_recv()
    lower = lane < 64
    odd_cell = lane // 32 % 2 == 1
    from_own = jnp.logical_xor(lower, jnp.logical_not(ahead))
    for j in range(2):
        plane = (quad * 2 + j).astype(jnp.float32)
        speed_x = jnp.abs((plane - (NV - 1) / 2.0) / NV)
        for h in range(4):
            rows = slice(8 * h, 8 * h + 8)
            own = adjoint[j, rows, :]
            second = beside[j, rows, :]
            first = jnp.where(from_own, pltpu.roll(own, 64, 1), pltpu.roll(second, 64, 1))
            partner = jnp.where(odd_cell, pltpu.roll(own, 32, 1), pltpu.roll(own, 96, 1))
            b = (lax.broadcasted_iota(jnp.int32, (8, 128), 0) + 8 * h).astype(jnp.float32)
            speed_y = jnp.abs((b - (NV - 1) / 2.0) / NV)
            passed_own[j, rows, :] = (
                own
                - speed_x * (3.0 * own - 4.0 * first + second) * 0.5
                - 2.0 * speed_y * (own - partner)
            )
        cells = exchange_lanes([passed_own[j, 8 * h : 8 * h + 8, :] for h in range(4)])
        for cell in range(4):
            passed_sent[cell, 8 * j : 8 * j + 8, :] = cells[cell]
    for_peers(lambda peer: to_peer(*passed_refs, peer).start())
    fold(1 - core)
    fold_loss()

    def tables(name):
        high, low = ROWS_OF[name]
        return table[high : high + 256, :], table[low : low + 256, :]

    def plane_of(ref, low_index):
        return ref[pl.ds(low_index, 32, stride=8), :]

    def tile_at(n):
        return slice(128 * n, 128 * n + 128)

    def factors():
        at = [slice(8 * n, 8 * n + 8) for n in range(16)]
        return [(twiddles[at[2 * n], :], twiddles[at[2 * n + 1], :]) for n in range(1, 8)]

    def load_eight(ref, rows):
        return [(ref[n, rows, :128], ref[n, rows, 128:]) for n in range(8)]

    def store_eight(ref, rows, values):
        for n, (re, im) in enumerate(values):
            ref[n, rows, :128] = re
            ref[n, rows, 128:] = im

    def eight_rows(start):
        return pl.ds(pl.multiple_of(start, 8), 8)

    def transform(planes, ref):
        left = table[LEFT_ROW : LEFT_ROW + 64, :96]
        mid = left_product(left, jnp.concatenate(planes, axis=1))
        rows = [
            jnp.concatenate([mid[:32, tile_at(n)], mid[32:, tile_at(n)]], axis=1) for n in range(8)
        ]
        ref[...] = product(jnp.concatenate(rows, axis=0), *tables("lanes")).reshape(8, NV, 256)

        def finish(r, carry):
            rows = eight_rows(8 * r)
            store_eight(ref, rows, forward_eight(load_eight(ref, rows), factors()))
            return carry

        lax.fori_loop(0, 4, finish, 0)

    def unfold(kind):
        def body(pair, carry):
            def tile_of(h, r):
                return gains[kind, eight_rows(pair * 32 + 8 * r), tile_at(h)]

            for h in (7, 6, 5, 4):
                for r in range(4):
                    values = mirrored(tile_of, h, r)
                    if h == 4:
                        values = jnp.where(lane < 32, tile_of(4, r), values)
                    upper[kind, eight_rows(pair * 32 + 8 * r), tile_at(h - 4)] = values
            return carry

        lax.fori_loop(0, 4, body, 0)

    for position in beside_columns:
        gain_arrival(position, core, gain_send, gain_recv).wait_recv()
        gain_arrival(position, core, share_send, share_recv).start()
    for position in beside_columns:
        gain_copy(2, loss_send, loss_recv, position).start()
    unfold(core)

    fetch_table.wait()
    fetch_twiddles.wait()
    all_of(*state_refs[1:]).wait_recv()
    transform([plane_of(state_all, n) for n in range(8)], spectrum)


    def wait_passed():
        all_of(*passed_refs[1:]).wait_recv()

    def transform_product():
        planes = [plane_of(state_all, n) * plane_of(passed_all, n) for n in range(8)]
        transform(planes, product_spectrum)

    wait_passed()
    transform_product()

    for position in beside_columns:
        gain_arrival(position, 1 - core, share_send, share_recv).wait_recv()
    unfold(1 - core)

    def gain_tile(kind, rows, n):
        return gains[kind, rows, tile_at(n)] if n < 4 else upper[kind, rows, tile_at(n - 4)]

    def filter_step(r, carry):
        rows = eight_rows(8 * r)
        both = []
        for n, (re, im) in enumerate(load_eight(spectrum, eight_rows(8 * lax.rem(r, 4)))):
            left, right = gain_tile(0, rows, n), gain_tile(1, rows, n)
            both.append((left * re - right * im, left * im + right * re))
        store_eight(work, rows, backward_eight(both, factors()))
        return carry

    lax.fori_loop(0, 16, filter_step, 0)

    def all_turned(values):
        parts = [turned(values[tile_at(n)]) for n in range(values.shape[0] // 128)]
        return jnp.concatenate(parts, axis=0)

    for i in range(0, 8, BLOCK):
        half = product(work[i : i + BLOCK].reshape(BLOCK * 128, 256), *tables("lanes_back"))
        fields = product(all_turned(half), *tables("slots_back"))
        work[i : i + BLOCK] = fields.reshape(BLOCK, 128, 256)

    for i in range(0, 8, BLOCK):
        crossed = []
        for n in range(i, i + BLOCK):
            weights = jnp.concatenate([plane_of(passed_all, n)] * 4, axis=0).T
            fields = work[n]
            crossed.append(
                jnp.concatenate([fields[:, 128:] * weights, fields[:, :128] * weights], axis=1)
            )
        half = product(jnp.concatenate(crossed, axis=0), *tables("slots"))
        fields = product(all_turned(half), *tables("lanes"))
        work[i : i + BLOCK] = fields.reshape(BLOCK, 128, 256)

    for position in beside_columns:
        gain_arrival(position, 2, loss_send, loss_recv).wait_recv()

    def loss_tile(h, r):
        return loss_gain[8 * r : 8 * r + 8, tile_at(h)]

    for r in range(4):
        for h in range(5):
            starts = [32 * pair + 8 * r for pair in range(4)]
            b = [gains[2, start : start + 8, tile_at(h)] for start in starts]
            loss_gain[8 * r : 8 * r + 8, tile_at(h)] = (b[0] + b[1]) + (b[2] + b[3])
    for h in (7, 6, 5, 4):
        for r in range(4):
            values = mirrored(loss_tile, h, r)
            if h == 4:
                values = jnp.where(lane < 32, loss_tile(4, r), values)
            loss_upper[8 * r : 8 * r + 8, tile_at(h - 4)] = values

    def total_step(r, carry):
        rows = eight_rows(8 * r)
        sums = []
        weights = [loss_gain[rows, tile_at(n)] for n in range(4)]
        weights += [loss_upper[rows, tile_at(n)] for n in range(4)]
        for n, (re, im) in enumerate(load_eight(product_spectrum, rows)):
            sums.append((-weights[n] * re, -weights[n] * im))
        for pair in range(4):
            at = eight_rows(32 * pair + 8 * r)
            for n, (re, im) in enumerate(forward_eight(load_eight(work, at), factors())):
                left, right = gain_tile(0, at, n), gain_tile(1, at, n)
                sums[n] = (
                    sums[n][0] + (left * re + right * im),
                    sums[n][1] + (left * im - right * re),
                )
        store_eight(total, rows, backward_eight(sums, factors()))
        lost = [
            (weights[n] * re, weights[n] * im)
            for n, (re, im) in enumerate(load_eight(spectrum, rows))
        ]
        store_eight(loss, rows, backward_eight(lost, factors()))
        return carry

    lax.fori_loop(0, 4, total_step, 0)

    both = jnp.concatenate([total[...].reshape(256, 256), loss[...].reshape(256, 256)], axis=0)
    both = product(both, *tables("lanes_back"))

    def last_axis(values):
        parts = [values[32 * n : 32 * n + 32] for n in range(8)]
        re = jnp.concatenate([part[:, :128] for part in parts], axis=1)
        im = jnp.concatenate([part[:, 128:] for part in parts], axis=1)
        left = table[LEFT_BACK_ROW : LEFT_BACK_ROW + 32, :192]
        return left_product(left, jnp.concatenate([re, im], axis=0))

    gained, lost = last_axis(both[:256]), last_axis(both[256:])
    for n in range(8):
        value = gained[:, tile_at(n)] - plane_of(passed_all, n) * lost[:, tile_at(n)]
        result[pl.ds(n, 32, stride=8), :] = value

    def result_copy(peer):
        return pltpu.make_async_remote_copy(
            src_ref=result.at[pl.ds(peer * 16, 16), :],
            dst_ref=arrived.at[pl.ds(quad * 16, 16), :],
            send_sem=result_send,
            recv_sem=result_recv,
            device_id={"tile": partner_tile, "quad": peer},
            device_id_type=MESH,
        )

    for_peers(lambda peer: result_copy(peer).start())

    halo.wait_send()
    all_of(*state_refs[1:]).wait_send()
    all_of(*passed_refs[1:]).wait_send()
    for position in beside_columns:
        gain_copy(core, gain_send, gain_recv, position).wait_send()
        gain_copy(2, loss_send, loss_recv, position).wait_send()
        gain_arrival(position, core, share_send, share_recv).wait_send()

    all_of(arrived, result_send, result_recv).wait_recv()

    def arrived_at(source, j):
        return arrived[16 * source + 8 * j : 16 * source + 8 * j + 8, :]

    for j in range(2):
        cells = [
            (arrived_at(cell, j) + arrived_at(4 + cell, j))
            + (arrived_at(8 + cell, j) + arrived_at(12 + cell, j))
            for cell in range(4)
        ]
        parts = exchange_lanes(cells)
        for h in range(4):
            part = slice(8 * h, 8 * h + 8)
            out[j, part, :] = passed_own[j, part, :] + parts[h] * (1.0 / 16.0)

    all_of(arrived, result_send, result_recv).wait_send()


def local(adjoint_next, saved_state, gain_left, gain_right):
    share = adjoint_next.shape
    whole_field = pltpu.VMEM((8, 128, 256), jnp.float32)
    one_field = pltpu.VMEM((8, NV, 256), jnp.float32)
    dma = pltpu.SemaphoreType.DMA
    in_vmem = pl.BlockSpec(memory_space=pltpu.VMEM)
    anywhere = pl.BlockSpec(memory_space=pl.ANY)
    table = jnp.asarray(make_tables())
    return pl.pallas_call(
        kernel,
        out_shape=jax.ShapeDtypeStruct(share, jnp.float32),
        in_specs=[anywhere] * 6,
        out_specs=in_vmem,
        scratch_shapes=[
            pltpu.VMEM((TABLE_ROWS, 256), jnp.bfloat16),
            pltpu.VMEM((128, 128), jnp.float32),
            pltpu.VMEM(share, jnp.float32),
            pltpu.VMEM(share, jnp.float32),
            pltpu.VMEM(share, jnp.float32),
            pltpu.VMEM(share, jnp.float32),
            pltpu.VMEM((4, 16, 128), jnp.float32),
            pltpu.VMEM((4, 16, 128), jnp.float32),
            pltpu.VMEM((256, 128), jnp.float32),
            pltpu.VMEM((256, 128), jnp.float32),
            pltpu.VMEM((256, 128), jnp.float32),
            pltpu.VMEM((256, 128), jnp.float32),
            pltpu.VMEM((2, NV, 1024), jnp.float32),
            pltpu.VMEM((3, 128, HALF), jnp.float32),
            pltpu.VMEM((2, 128, 512), jnp.float32),
            pltpu.VMEM((NV, HALF), jnp.float32),
            pltpu.VMEM((NV, 512), jnp.float32),
            one_field,
            one_field,
            one_field,
            one_field,
            whole_field,
            dma((6,)),
            dma((2,)),
            dma,
            dma,
            dma,
            dma,
            dma,
            dma,
            dma((4,)),
            dma((4,)),
            dma((4,)),
            dma((4,)),
            dma((4,)),
            dma((4,)),
            pltpu.SemaphoreType.REGULAR,
            pltpu.SemaphoreType.REGULAR,
        ],
        compiler_params=pltpu.CompilerParams(
            collective_id=0, has_side_effects=True, vmem_limit_bytes=60 * 1024 * 1024
        ),
        name="adjoint_step",
    )(adjoint_next, saved_state, gain_left, gain_right, table, jnp.asarray(make_twiddles()))


def solution(mesh):
    in_specs = (
        P("quad", None, "tile"),
        P("quad", None, "tile"),
        P("quad", None, None),
        P("quad", None, None),
    )
    out_specs = P("quad", None, "tile")
    return jax.shard_map(local, mesh=mesh, in_specs=in_specs, out_specs=out_specs, check_vma=False)
```
